32 devices in a mesh: outer: 8 (over z, y), narrow: 4 (over x, core).
Axes of the slice: x: 2, y: 2, z: 4, core: 2. Of those that a mesh axis runs over, the one named last changes fastest.
Arguments:
- queries: bfloat16 [8192, 4096], P(('outer', 'narrow')), may hold values from -6 to 6
- keys: bfloat16 [8192, 4096], P(('outer', 'narrow')), may hold values from -6 to 6
- values: bfloat16 [8192, 4096], P(('outer', 'narrow')), may hold values from -6 to 6
- log_decay: float32 [32, 8192], P(None, ('outer', 'narrow')), may hold values from -0.8 to 0
- gain: float32 [4096], replicated, may hold values from 0.5 to 1.5
Outputs:
- mixed: bfloat16 [8192, 4096], P(('outer', 'narrow'))
The draws below stay inside these ranges and needn't reach their ends.
All inputs are finite; a program needn't handle non-finite values.
Results may differ from the reference program's by a relative error of at most 0.0052.
Values may be sent and summed in bfloat16 or wider, within the bound.
A program may use at most 64 MiB of HBM per device.

```python
import jax
import jax.numpy as jnp
from jax import lax

HEAD_COUNT = 32
DH = 128
TOK_DEV = 256
D = 4096
SPAN_LENGTH = 8192


def draw_log_decay(key, part):
    segments = jax.random.split(jax.random.fold_in(key, 17), 7)
    share = 0.5
    fast = jax.random.uniform(segments[0], (HEAD_COUNT,), jnp.float32) < share
    horizon = jnp.exp(jax.random.uniform(segments[1], (HEAD_COUNT,), jnp.float32, jnp.log(30.0), jnp.log(50.0)))
    slow_total = jax.random.uniform(segments[2], (HEAD_COUNT,), jnp.float32, 0.1, 0.3)
    base = jnp.where(fast, -1.0 / horizon, -slow_total / SPAN_LENGTH)
    count = SPAN_LENGTH // TOK_DEV
    block_factor = jnp.exp(jax.random.uniform(segments[3], (HEAD_COUNT, count), jnp.float32, jnp.log(0.5), jnp.log(2.0)))
    block_factor = jnp.repeat(block_factor, TOK_DEV, axis=1)
    place_factor = jax.random.uniform(segments[4], (HEAD_COUNT, SPAN_LENGTH), jnp.float32, 0.5, 1.5)
    forget_speeds = base[:, None] * block_factor * place_factor
    spike_indices = jax.random.randint(segments[5], (HEAD_COUNT, 2), 0, SPAN_LENGTH)
    forget_falls = jax.random.uniform(segments[6], (HEAD_COUNT, 2), jnp.float32, jnp.log(0.5), jnp.log(0.8))
    spike_finder = jnp.arange(SPAN_LENGTH)[None, None, :] == spike_indices[:, :, None]
    forget_spikes = jnp.sum(jnp.where(spike_finder, forget_falls[:, :, None], 0.0), axis=1)
    return (forget_speeds + forget_spikes).astype(jnp.float32)


def block_levels(key, extent, shards, least, largest):
    factor_of, own = 1.0, jax.random.fold_in(key, 6)
    for axis_at, shards_of in shards:
        steps = jnp.exp(jax.random.uniform(jax.random.fold_in(own, axis_at), (shards_of,), jnp.float32, least / len(shards), largest / len(shards)))
        factor_of = factor_of * jnp.repeat(steps, extent[axis_at] // shards_of).reshape([-1 if axis == axis_at else 1 for axis in range(len(extent))])
    return factor_of


def scatter_about(key, dims, scale, reach, pieces=(), kind=jnp.bfloat16):
    array = scale * jax.random.normal(key, dims, jnp.float32)
    if pieces:
        array = array * block_levels(key, dims, pieces, -0.22, 0.18)
    return jnp.clip(array, -reach, reach).astype(kind)


def setup_inputs(seed: int = 0) -> dict:
    key_list = jax.random.split(jax.random.key(seed), 6)
    queries = scatter_about(key_list[0], (SPAN_LENGTH, D), 1.0, 6.0, ((0, 32),))
    keys = scatter_about(key_list[1], (SPAN_LENGTH, D), 1.0, 6.0, ((0, 32),))
    values = scatter_about(key_list[2], (SPAN_LENGTH, D), 1.0, 6.0, ((0, 32),))
    log_decay = draw_log_decay(jax.random.fold_in(key_list[5], 71), 0)
    gain = jnp.clip(1.0 + 0.1 * jax.random.normal(key_list[4], (D,), jnp.float32), 0.5, 1.5)
    return {"queries": queries, "keys": keys, "values": values, "log_decay": log_decay, "gain": gain}


def reference(queries, keys, values, log_decay, gain):
    blocks = queries.shape[0] // TOK_DEV
    qall = queries.reshape(blocks, TOK_DEV, HEAD_COUNT, DH)
    kall = keys.reshape(blocks, TOK_DEV, HEAD_COUNT, DH)
    vall = values.reshape(blocks, TOK_DEV, HEAD_COUNT, DH)
    decay_all = jnp.transpose(log_decay.reshape(HEAD_COUNT, blocks, TOK_DEV), (1, 0, 2))
    gains = gain.reshape(HEAD_COUNT, DH)
    causal = jnp.arange(TOK_DEV)[:, None] >= jnp.arange(TOK_DEV)[None, :]

    def step(state, inputs):
        qblk, kblk, vblk, forget_speeds = inputs
        cum = jnp.cumsum(forget_speeds, axis=1)
        total = cum[:, -1]
        factor = jnp.exp(total[:, None] - cum).T
        decayed = (kblk.astype(jnp.float32) * factor[:, :, None]).astype(jnp.bfloat16)
        block_state = jnp.einsum('thd,the->hde', decayed.astype(jnp.float32), vblk.astype(jnp.float32))
        half = state.astype(jnp.bfloat16)
        scores = jnp.einsum('thd,shd->hts', qblk.astype(jnp.float32), kblk.astype(jnp.float32))
        spread = jnp.minimum(cum[:, :, None] - cum[:, None, :], 0.0)
        weights = jnp.where(causal[None], scores * jnp.exp(spread), 0.0).astype(jnp.bfloat16)
        inner = jnp.einsum('hts,she->the', weights.astype(jnp.float32), vblk.astype(jnp.float32))
        readout = jnp.einsum('thd,hde->the', qblk.astype(jnp.float32), half.astype(jnp.float32))
        numer = inner + readout * jnp.exp(cum).T[:, :, None]
        scale = lax.rsqrt(lax.optimization_barrier(jnp.mean(numer * numer, axis=-1, keepdims=True)) + 1e-06)
        result = (numer * scale * gains[None]).astype(jnp.bfloat16)
        fresh = jnp.exp(total)[:, None, None] * state + block_state
        return (fresh, result.reshape(TOK_DEV, HEAD_COUNT * DH))
    start = jnp.zeros((HEAD_COUNT, DH, DH), jnp.float32)
    final, outputs = lax.scan(step, start, (qall, kall, vall, decay_all))
    return outputs.reshape(blocks * TOK_DEV, HEAD_COUNT * DH)
```

```python
import functools

import jax
import jax.numpy as jnp
from jax import lax
from jax.experimental import pallas as pl
from jax.experimental.pallas import tpu as pltpu
from jax.sharding import PartitionSpec as P

MESH = pl.DeviceIdType.MESH
FAR = -1e30


def split_outer(outer):
    rows = 1
    for d in range(1, outer + 1):
        if d * d <= outer and outer % d == 0:
            rows = d
    return outer // rows, rows


def kernel(
    sizes, q_hbm, k_hbm, v_hbm, ld_hbm, gain_hbm, out_hbm,
    q_ref, k_ref, v_ref, ld_ref, gain_ref, out_ref, cum, decay_cols, tail_cols, head_cols, bias, inner,
    made, got1, t1, wsend, got2, t2, got3, t3, gsend, got4, csend, carried,
    load_sem, out_sem, send_sem, recv_sem, tsend_sem, trecv_sem,
):
    narrow, depth, rows, heads, width, unit = sizes
    tokens = q_ref.shape[0]
    own = heads // narrow
    chunks = own // rows
    o, n = lax.axis_index("outer"), lax.axis_index("narrow")
    z, y = o // rows, lax.rem(o, rows)

    near = [lax.rem(n + i % narrow, narrow) for i in range(narrow // 2, narrow // 2 + narrow) if i % narrow]
    level = [lax.rem(y + i, rows) for i in range(1, rows)]
    deep = [lax.rem(z + i, depth) for i in range(1, depth)]
    group_at = lambda j: (o, j)
    row_at = lambda j: (z * rows + j, n)
    depth_at = lambda j: (j * rows + y, n)

    loads = [
        pltpu.make_async_copy(src, dst, load_sem.at[i])
        for i, (src, dst) in enumerate(
            ((ld_hbm, ld_ref), (k_hbm, k_ref), (v_hbm, v_ref), (q_hbm, q_ref), (gain_hbm, gain_ref))
        )
    ]
    for one in loads:
        one.start()

    barrier = pltpu.get_barrier_semaphore()
    peers = [group_at(j) for j in near] + [row_at(j) for j in level] + [depth_at(j) for j in deep]
    for peer in peers:
        pl.semaphore_signal(barrier, inc=1, device_id=peer, device_id_type=MESH)

    loads[0].wait()
    total = ld_ref[...]
    lane = lax.broadcasted_iota(jnp.int32, total.shape, 1)
    step = 1
    while step < tokens:
        total = total + jnp.where(lane >= step, pltpu.roll(total, step, axis=1), 0.0)
        step *= 2
    cum[...] = total
    t1[n] = jnp.broadcast_to(total[:, tokens - 1 :], (heads, width))
    cols = jnp.concatenate([total, jnp.zeros((128 - heads, tokens), jnp.float32)], axis=0).T
    tail = jnp.exp(cols[tokens - 1 :] - cols)
    grown = jnp.exp(cols)
    for g in range(heads // unit):
        shift = (128 - g * unit) % 128
        for ref, value in ((decay_cols, cols), (tail_cols, tail), (head_cols, grown)):
            ref[g] = pltpu.roll(value, shift, axis=1) if shift else value
    at_t = lax.broadcasted_iota(jnp.int32, (tokens, tokens), 0)
    at_s = lax.broadcasted_iota(jnp.int32, (tokens, tokens), 1)
    bias[...] = jnp.where(at_t >= at_s, 0.0, FAR)

    def lanes(h):
        return pl.ds(pl.multiple_of(h * width, width), width)

    def states(c):
        def body(j, _):
            for r in range(rows):
                k = c * rows + r
                at = lanes(j * own + k)
                tails = tail_cols[j * (own // unit) + k // unit]
                u = k % unit
                kept = k_ref[:, at].astype(jnp.float32) * tails[:, u : u + 1]
                made[c, j, r] = lax.dot_general(
                    kept.astype(jnp.bfloat16), v_ref[:, at], (((0,), (0,)), ((), ())),
                    preferred_element_type=jnp.float32,
                ).astype(jnp.bfloat16)
            return 0

        lax.fori_loop(0, narrow, body, 0, unroll=2)

    def within(first, last):
        def body(g, _):
            columns = decay_cols[g]
            for u in range(unit):
                h = g * unit + u
                at = lanes(h)
                scores = lax.dot_general(
                    q_ref[:, at], k_ref[:, at], (((1,), (1,)), ((), ())),
                    preferred_element_type=jnp.float32,
                )
                spread = columns[:, u : u + 1] - cum[pl.ds(h, 1), :] + bias[...]
                weights = (scores * jnp.exp(spread)).astype(jnp.bfloat16)
                inner[:, at] = jnp.dot(weights, v_ref[:, at], preferred_element_type=jnp.float32)
            return 0

        lax.fori_loop(first, last, body, 0)

    def finish(c, j):
        for r in range(rows):
            k = c * rows + r
            at = lanes(j * own + k)
            grow = head_cols[j * (own // unit) + k // unit]
            u = k % unit
            read = jnp.dot(q_ref[:, at], carried[c, j, r], preferred_element_type=jnp.float32)
            numer = inner[:, at] + read * grow[:, u : u + 1]
            mean = jnp.mean(numer * numer, axis=-1, keepdims=True)
            out_ref[:, at] = (numer * lax.rsqrt(mean + 1e-06) * gain_ref[:, at]).astype(jnp.bfloat16)

    pending, stored = [], []

    def begin(kind, c, src, dst, peers_of, where, mine):
        for i, j in enumerate(peers_of):
            one = pltpu.make_async_remote_copy(
                src_ref=src(j), dst_ref=dst(mine), send_sem=send_sem.at[kind, c, i],
                recv_sem=recv_sem.at[kind, c, mine], device_id=where(j), device_id_type=MESH,
            )
            one.start()
            pending.append(one)

    def arrive(kind, c, dst, peers_of, where):
        for i, j in enumerate(peers_of):
            pltpu.make_async_remote_copy(
                src_ref=dst(j), dst_ref=dst(j), send_sem=send_sem.at[kind, c, i],
                recv_sem=recv_sem.at[kind, c, j], device_id=where(j), device_id_type=MESH,
            ).wait_recv()

    def begin_total(kind, ref, mine, peers_of, where):
        for i, j in enumerate(peers_of):
            one = pltpu.make_async_remote_copy(
                src_ref=ref.at[mine], dst_ref=ref.at[mine], send_sem=tsend_sem.at[kind, i],
                recv_sem=trecv_sem.at[kind, mine], device_id=where(j), device_id_type=MESH,
            )
            one.start()
            pending.append(one)

    def arrive_total(kind, ref, peers_of, where):
        for i, j in enumerate(peers_of):
            pltpu.make_async_remote_copy(
                src_ref=ref.at[j], dst_ref=ref.at[j], send_sem=tsend_sem.at[kind, i],
                recv_sem=trecv_sem.at[kind, j], device_id=where(j), device_id_type=MESH,
            ).wait_recv()

    def decay(ref, j, k):
        return jnp.exp(ref[j, pl.ds(n * own + k, 1), :])

    def stage0(c):
        states(c)
        begin(0, c, lambda j: made.at[c, j], lambda j: got1.at[c, j], near, group_at, n)
        got1[c, n] = made[c, n]

    def stage1(c):
        arrive(0, c, lambda j: got1.at[c, j], near, group_at)
        for r in range(rows):
            acc = got1[c, 0, r].astype(jnp.float32)
            for j in range(1, narrow):
                acc = decay(t1, j, c * rows + r) * acc + got1[c, j, r].astype(jnp.float32)
            wsend[c, r] = acc.astype(jnp.bfloat16)
        begin(1, c, lambda j: wsend.at[c, j], lambda j: got2.at[c, j], level, row_at, y)
        got2[c, y] = wsend[c, y]

    def stage2(c):
        arrive(1, c, lambda j: got2.at[c, j], level, row_at)
        acc = got2[c, 0].astype(jnp.float32)
        for j in range(1, rows):
            acc = decay(t2, j, c * rows + y) * acc + got2[c, j].astype(jnp.float32)
        got3[c, z] = acc.astype(jnp.bfloat16)
        begin(2, c, lambda j: got3.at[c, z], lambda j: got3.at[c, j], deep, depth_at, z)

    def stage3(c):
        arrive(2, c, lambda j: got3.at[c, j], deep, depth_at)
        k = c * rows + y
        acc = jnp.zeros((width, width), jnp.float32)
        for j in range(depth - 1):
            new = decay(t3, j, k) * acc + got3[c, j].astype(jnp.float32)
            acc = jnp.where(j < z, new, acc)
        for j in range(rows):
            gsend[c, j] = acc.astype(jnp.bfloat16)
            if j < rows - 1:
                acc = decay(t2, j, k) * acc + got2[c, j].astype(jnp.float32)
        begin(3, c, lambda j: gsend.at[c, j], lambda j: got4.at[c, j], level, row_at, y)
        got4[c, y] = gsend[c, y]

    def stage4(c):
        arrive(3, c, lambda j: got4.at[c, j], level, row_at)
        for r in range(rows):
            acc = got4[c, r].astype(jnp.float32)
            for j in range(narrow):
                csend[c, j, r] = acc.astype(jnp.bfloat16)
                if j < narrow - 1:
                    acc = decay(t1, j, c * rows + r) * acc + got1[c, j, r].astype(jnp.float32)
        begin(4, c, lambda j: csend.at[c, j], lambda j: carried.at[c, j], near, group_at, n)
        carried[c, n] = csend[c, n]

    def stage5(c):
        arrive(4, c, lambda j: carried.at[c, j], near, group_at)

        def body(j, _):
            finish(c, j)
            return 0

        lax.fori_loop(0, narrow, body, 0, unroll=2)
        for j in range(narrow):
            at = pl.ds((j * own + c * rows) * width, rows * width)
            one = pltpu.make_async_copy(out_ref.at[:, at], out_hbm.at[:, at], out_sem.at[c, j])
            one.start()
            stored.append(one)

    def totals1():
        arrive_total(0, t1, near, group_at)
        group_total = t1[0]
        for j in range(1, narrow):
            group_total = group_total + t1[j]
        t2[y] = group_total
        begin_total(1, t2, y, level, row_at)

    def totals2():
        arrive_total(1, t2, level, row_at)
        row_total = t2[0]
        for j in range(1, rows):
            row_total = row_total + t2[j]
        t3[z] = row_total
        begin_total(2, t3, z, deep, depth_at)

    pl.semaphore_wait(barrier, len(peers))
    begin_total(0, t1, n, near, group_at)
    loads[1].wait()
    loads[2].wait()
    for c in range(chunks):
        stage0(c)
    totals1()
    loads[3].wait()
    loads[4].wait()

    groups = heads // unit
    events = [(TIMES[p] + GAP * c, p, c) for p in range(5) for c in range(chunks)]
    events += [(TIMES[1] - 0.1, 5, 0), (TIMES[2] - 0.1, 6, 0)]
    early = min(groups, EARLY)
    within(0, early)
    filled = early
    for _, p, c in sorted(events):
        if p == 4 and filled < groups:
            within(filled, groups)
            filled = groups
        if p == 5:
            totals2()
        elif p == 6:
            arrive_total(2, t3, deep, depth_at)
        else:
            (stage1, stage2, stage3, stage4, stage5)[p](c)
            if filled < groups:
                within(filled, filled + 1)
                filled += 1
    for one in pending:
        one.wait_send()
    for one in stored:
        one.wait()


TIMES = (5.4, 7.8, 12.8, 15.2, 19.6)
GAP = 2.75
EARLY = 2


def on_device(mesh_sizes, queries, keys, values, log_decay, gain):
    outer, narrow = mesh_sizes
    tokens, model = queries.shape
    heads = log_decay.shape[0]
    width = model // heads
    depth, rows = split_outer(outer)
    own = heads // narrow
    chunks = own // rows
    unit = min(4, own)
    half = lambda *shape: pltpu.VMEM(shape + (width, width), jnp.bfloat16)
    full = lambda *shape: pltpu.VMEM(shape, jnp.float32)
    most = max(narrow, depth, rows)
    dma = lambda *shape: pltpu.SemaphoreType.DMA(shape)
    hbm = pl.BlockSpec(memory_space=pltpu.HBM)
    return pl.pallas_call(
        functools.partial(kernel, (narrow, depth, rows, heads, width, unit)),
        out_shape=jax.ShapeDtypeStruct(queries.shape, jnp.bfloat16),
        in_specs=[hbm] * 5,
        out_specs=hbm,
        scratch_shapes=[
            pltpu.VMEM((tokens, model), queries.dtype),
            pltpu.VMEM((tokens, model), queries.dtype),
            pltpu.VMEM((tokens, model), queries.dtype),
            full(heads, tokens),
            full(1, model),
            pltpu.VMEM((tokens, model), queries.dtype),
            full(heads, tokens),
            full(heads // unit, tokens, 128),
            full(heads // unit, tokens, 128),
            full(heads // unit, tokens, 128),
            full(tokens, tokens),
            full(tokens, model),
            half(chunks, narrow, rows),
            half(chunks, narrow, rows),
            full(narrow, heads, width),
            half(chunks, rows),
            half(chunks, rows),
            full(rows, heads, width),
            half(chunks, depth),
            full(depth, heads, width),
            half(chunks, rows),
            half(chunks, rows),
            half(chunks, narrow, rows),
            half(chunks, narrow, rows),
            dma(5),
            dma(chunks, narrow),
            dma(5, chunks, most),
            dma(5, chunks, most),
            dma(3, most),
            dma(3, most),
        ],
        compiler_params=pltpu.CompilerParams(
            collective_id=0, has_side_effects=True, vmem_limit_bytes=67_000_000
        ),
    )(queries, keys, values, log_decay, gain.reshape(1, model))


def solution(mesh):
    axes = ("outer", "narrow")
    block = P(axes, None)
    return jax.shard_map(
        functools.partial(on_device, tuple(mesh.shape[a] for a in axes)),
        mesh=mesh,
        in_specs=(block, block, block, P(None, axes), P()),
        out_specs=block,
        check_vma=False,
    )
```

```python
import functools

import jax
import jax.numpy as jnp
from jax import lax
from jax.experimental import pallas as pl
from jax.experimental.pallas import tpu as pltpu
from jax.sharding import PartitionSpec as P

MESH = pl.DeviceIdType.MESH
FAR = -1e30
CORES = 2
PARTS = 2
EARLY = 3
LAG_Z = 4
LAG_R = 8


def split_outer(outer):
    rows = 1
    for d in range(1, outer + 1):
        if d * d <= outer and outer % d == 0:
            rows = d
    return outer // rows, rows


def kernel(
    sizes, q_hbm, k_hbm, v_hbm, ld_hbm, gain_hbm, out_ref,
    q_ref, k_ref, v_ref, ld_ref, gain_ref, cum, decay_cols, tail_cols, bias, inner, grown,
    tcore, dcore, ptot, tin, dchip, tz, dz, down,
    made, pair, tsend, got_t, q_sum, zsend, got_z, rsend, got_r, own_c, csend, got_c,
    load_sem, made_send, made_recv, ct_send, ct_recv, t_send, t_recv, pt_send, pt_recv,
    zt_send, zt_recv, z_send, z_recv, r_send, r_recv, c_send, c_recv, ready,
):
    depth, rows, across, heads, width, per = sizes
    chips = rows * across
    levels = max(depth - 1, 1).bit_length() if depth > 1 else 0
    tokens = q_ref.shape[0]
    part = width // PARTS
    units = per * PARTS
    o, n = lax.axis_index("outer"), lax.axis_index("narrow")
    z, y = o // rows, lax.rem(o, rows)
    x, core = n // CORES, lax.rem(n, CORES)
    me = y * across + x
    first = core == 0

    partner = (o, x * CORES + 1 - core)
    chip_at = lambda p: (z * rows + p // across, lax.rem(p, across) * CORES + core)
    plane_at = lambda j: (j * rows + y, n)
    beside = lambda i: lax.rem(me + i, chips)
    slot = lambda p: lax.rem(p - me - 1 + chips, chips)

    loads = [
        pltpu.make_async_copy(src, dst, load_sem.at[i])
        for i, (src, dst) in enumerate(
            ((ld_hbm, ld_ref), (k_hbm, k_ref), (v_hbm, v_ref), (q_hbm, q_ref), (gain_hbm, gain_ref))
        )
    ]
    for one in loads:
        one.start()

    barrier = pltpu.get_barrier_semaphore()
    pl.semaphore_signal(barrier, inc=1, device_id=partner, device_id_type=MESH)
    for i in range(1, chips):
        pl.semaphore_signal(barrier, inc=1, device_id=chip_at(beside(i)), device_id_type=MESH)
    for j in range(1, depth):
        @pl.when(j > z)
        def _():
            pl.semaphore_signal(barrier, inc=1, device_id=plane_at(j), device_id_type=MESH)

    def remote(src, dst, send, recv, where):
        return pltpu.make_async_remote_copy(
            src_ref=src, dst_ref=dst, send_sem=send, recv_sem=recv, device_id=where, device_id_type=MESH
        )

    def arrived(ref, recv):
        remote(ref, ref, made_send, recv, partner).wait_recv()

    def sent(ref, send):
        remote(ref, ref, send, ct_recv, partner).wait_send()

    loads[0].wait()
    total = ld_ref[...]
    lane = lax.broadcasted_iota(jnp.int32, total.shape, 1)
    step = 1
    while step < tokens:
        total = total + jnp.where(lane >= step, pltpu.roll(total, step, axis=1), 0.0)
        step *= 2
    cum[...] = total
    last = jnp.broadcast_to(total[:, tokens - 1 :], (heads, width))
    for g in range(heads // per):
        tcore[core, g, :per, :] = last[g * per : (g + 1) * per]
    cols = jnp.concatenate([total, jnp.zeros((128 - heads, tokens), jnp.float32)], axis=0).T
    tail = jnp.exp(cols[tokens - 1 :] - cols)
    for g in range(heads // per):
        shift = (128 - g * per) % 128
        tail_cols[g] = pltpu.roll(tail, shift, axis=1) if shift else tail

    def lanes(h):
        return pl.ds(pl.multiple_of(h * width, width), width)

    def state(c, p, a):
        g = p * CORES + a
        at = lanes(g * per + c)
        kept = k_ref[:, at].astype(jnp.float32) * tail_cols[g][:, c : c + 1]
        return lax.dot_general(
            kept.astype(jnp.bfloat16), v_ref[:, at], (((0,), (0,)), ((), ())),
            preferred_element_type=jnp.float32,
        ).astype(jnp.bfloat16)

    def states(c, mine):
        def body(p, _):
            made_here = state(c, p, core if mine else 1 - core)
            for f in range(PARTS):
                piece = made_here[f * part : (f + 1) * part]
                if mine:
                    pair[core, c, f, p] = piece
                else:
                    made[c, f, p] = piece
            return 0

        lax.fori_loop(0, chips, body, 0, unroll=2 if chips % 2 == 0 else 1)

    def meet(c):
        arrived(pair.at[1 - core, c], made_recv.at[c])
        for f in range(PARTS):
            for p in range(chips):
                decay = dcore[1, p, pl.ds(c, 1), :]
                value = decay * pair[0, c, f, p].astype(jnp.float32) + pair[1, c, f, p].astype(jnp.float32)
                tsend[c, f, slot(p)] = value.astype(jnp.bfloat16)
            for i in range(1, chips):
                remote(
                    tsend.at[c, f, i - 1], got_t.at[c, f, chips - 1 - i], t_send,
                    t_recv.at[c * PARTS + f], chip_at(beside(i)),
                ).start()

    def meet_totals():
        arrived(tcore.at[1 - core], ct_recv)
        for p in range(chips):
            here = [tcore[k, p * CORES + core] for k in range(CORES)]
            for k in range(CORES):
                dcore[k, p] = jnp.exp(here[k])
            ptot[slot(p)] = here[0] + here[1]
        for i in range(1, chips):
            remote(ptot.at[i - 1], tin.at[chips - 1 - i], pt_send, pt_recv, chip_at(beside(i))).start()

    def within(g):
        columns = decay_cols[g]
        for u in range(per):
            h = g * per + u
            at = lanes(h)
            spread_t = jnp.broadcast_to(columns[:, u : u + 1], (tokens, width))
            grown[h] = jnp.exp(spread_t)
            scores = lax.dot_general(
                q_ref[:, at], k_ref[:, at], (((1,), (1,)), ((), ())),
                preferred_element_type=jnp.float32,
            )
            spread = columns[:, u : u + 1] - cum[pl.ds(h, 1), :] + bias[...]
            weights = (scores * jnp.exp(spread)).astype(jnp.bfloat16)
            inner[:, at] = jnp.dot(weights, v_ref[:, at], preferred_element_type=jnp.float32)

    def send_level(level, s):
        for i in range(2**level):
            @pl.when(z + 1 + i < depth)
            def _():
                remote(
                    zsend.at[s], got_z.at[level, s], z_send.at[i], z_recv.at[level, s], plane_at(z + 1 + i)
                ).start()

    def sends_at(level):
        return lax.rem(z, 2 ** (level + 1)) == 2**level - 1

    def plane_totals():
        if chips > 1:
            arrived(tin.at[pl.ds(0, chips - 1)], pt_recv)
        tin[chips - 1] = ptot[chips - 1]
        whole = jnp.zeros_like(tz[0])
        for p in range(chips):
            here = tin[slot(p)]
            dchip[p] = jnp.exp(here)
            whole = whole + here
        tz[z] = whole
        down[...] = jnp.exp(whole)
        if depth > 1:
            @pl.when(z < depth - 1)
            def _():
                pl.semaphore_wait(ready, depth - 1 - z)
            for i in range(1, depth):
                @pl.when(z + i < depth)
                def _():
                    remote(tz.at[z], tz.at[z], zt_send.at[i - 1], zt_recv.at[z], plane_at(z + i)).start()

    def plane(s):
        c, f = s // PARTS, lax.rem(s, PARTS)
        if chips > 1:
            arrived(got_t.at[c, f, pl.ds(0, chips - 1)], t_recv.at[s])
        got_t[c, f, chips - 1] = tsend[c, f, chips - 1]
        acc = got_t[c, f, slot(0)].astype(jnp.float32)
        for p in range(1, chips):
            acc = dchip[p, pl.ds(c, 1), :] * acc + got_t[c, f, slot(p)].astype(jnp.float32)
        q_sum[s] = acc
        if levels:
            @pl.when(sends_at(0))
            def _():
                zsend[s] = acc.astype(jnp.bfloat16)
                send_level(0, s)

    def depth_totals():
        for j in range(depth - 1):
            @pl.when(j < z)
            def _():
                arrived(tz.at[j], zt_recv.at[j])
        for k in range(1, levels):
            start = z // 2**k * 2**k
            whole = jnp.zeros_like(tz[0])
            for j in range(depth - 1):
                whole = whole + jnp.where((j >= start) & (j < z), tz[j], 0.0)
            dz[k] = jnp.exp(whole)

    def scan(s):
        c, f = s // PARTS, lax.rem(s, PARTS)
        acc = jnp.zeros((part, width), jnp.float32)
        for k in range(levels):
            odd = lax.rem(z // 2**k, 2) == 1

            @pl.when(odd)
            def _():
                arrived(got_z.at[k, s], z_recv.at[k, s])

            came = got_z[k, s].astype(jnp.float32)
            if k:
                came = dz[k, pl.ds(c, 1), :] * came + acc
            acc = jnp.where(odd, came, acc)
            if k + 1 < levels:
                @pl.when(sends_at(k + 1))
                def _():
                    zsend[s] = (down[pl.ds(c, 1), :] * acc + q_sum[s]).astype(jnp.bfloat16)
                    send_level(k + 1, s)
        for p in range(chips):
            rsend[c, f, slot(p)] = acc.astype(jnp.bfloat16)
            if p < chips - 1:
                acc = dchip[p, pl.ds(c, 1), :] * acc + got_t[c, f, slot(p)].astype(jnp.float32)
        for i in range(1, chips):
            remote(
                rsend.at[c, f, i - 1], got_r.at[c, f, chips - 1 - i], r_send, r_recv.at[s], chip_at(beside(i))
            ).start()

    def back(s):
        c, f = s // PARTS, lax.rem(s, PARTS)
        if chips > 1:
            arrived(got_r.at[c, f, pl.ds(0, chips - 1)], r_recv.at[s])
        got_r[c, f, chips - 1] = rsend[c, f, chips - 1]
        for p in range(chips):
            before = got_r[c, f, slot(p)]
            after = dcore[0, p, pl.ds(c, 1), :] * before.astype(jnp.float32) + pair[0, c, f, p].astype(jnp.float32)
            after = after.astype(jnp.bfloat16)
            own_c[c, f, p] = jnp.where(first, before, after)
            csend[c, f, p] = jnp.where(first, after, before)
        remote(csend.at[c, f], got_c.at[c, f], c_send, c_recv.at[c], partner).start()

    def finish(c, ref, a):
        def body(p, _):
            h = (p * CORES + a) * per + c
            at = lanes(h)
            carried = jnp.concatenate([ref[c, f, p] for f in range(PARTS)], axis=0)
            read = jnp.dot(q_ref[:, at], carried, preferred_element_type=jnp.float32)
            numer = inner[:, at] + read * grown[h]
            mean = jnp.mean(numer * numer, axis=-1, keepdims=True)
            out_ref[:, at] = (numer * lax.rsqrt(mean + 1e-06) * gain_ref[:, at]).astype(jnp.bfloat16)
            return 0

        lax.fori_loop(0, chips, body, 0, unroll=2 if chips % 2 == 0 else 1)

    loads[1].wait()
    loads[2].wait()
    states(0, False)
    pl.semaphore_wait(barrier, chips + z)
    if depth > 1:
        for j in range(depth - 1):
            @pl.when(j < z)
            def _():
                pl.semaphore_signal(ready, inc=1, device_id=plane_at(j), device_id_type=MESH)
    remote(tcore.at[core], tcore.at[core], ct_send, ct_recv, partner).start()
    for c in range(per):
        if c:
            states(c, False)
        remote(made.at[c], pair.at[core, c], made_send, made_recv.at[c], partner).start()
        if c:
            meet(c - 1)
        states(c, True)
        if c == 0:
            meet_totals()
    meet(per - 1)

    for g in range(heads // per):
        shift = (128 - g * per) % 128
        decay_cols[g] = pltpu.roll(cols, shift, axis=1) if shift else cols
    at_t = lax.broadcasted_iota(jnp.int32, (tokens, tokens), 0)
    at_s = lax.broadcasted_iota(jnp.int32, (tokens, tokens), 1)
    bias[...] = jnp.where(at_t >= at_s, 0.0, FAR)
    loads[3].wait()
    loads[4].wait()

    groups = heads // per
    early = min(EARLY, groups)
    lax.fori_loop(0, early, lambda g, _: (within(g), 0)[1], 0)
    plane_totals()

    rank = jnp.int32(0)
    for k in range(levels):
        rank = jnp.where(z >= 2**k, k + 1, rank)
    lag_z = jnp.minimum(rank * LAG_Z, units)
    lag_r = lag_z + LAG_R
    lag_f = lag_r + PARTS - 1
    steps = lag_f + units

    def step_at(s, _):
        @pl.when(s + early < groups)
        def _():
            within(s + early)

        @pl.when(s < units)
        def _():
            plane(s)

        if levels:
            @pl.when(s == lag_z)
            def _():
                depth_totals()

        @pl.when((s >= lag_z) & (s < lag_z + units))
        def _():
            scan(s - lag_z)

        @pl.when((s >= lag_r) & (s < lag_r + units))
        def _():
            back(s - lag_r)

        t = s - lag_f
        for f in range(PARTS):
            @pl.when((t >= 0) & (lax.rem(t + PARTS, PARTS) == f))
            def _():
                c = t // PARTS
                if f == 0:
                    finish(c, own_c, core)
                if f == PARTS - 1:
                    arrived(got_c.at[c], c_recv.at[c])
                    finish(c, got_c, 1 - core)
        return 0

    most = max(groups - early, units)
    lax.fori_loop(0, jnp.maximum(steps, most), step_at, 0)

    sent(made, made_send)
    sent(tcore.at[core], ct_send)
    if chips > 1:
        sent(tsend.at[:, :, pl.ds(0, chips - 1)], t_send)
        sent(ptot.at[pl.ds(0, chips - 1)], pt_send)
        sent(rsend.at[:, :, pl.ds(0, chips - 1)], r_send)
    sent(csend, c_send)
    for i in range(1, depth):
        @pl.when(z + i < depth)
        def _():
            sent(tz.at[z], zt_send.at[i - 1])
    for level in range(levels):
        for i in range(2**level):
            @pl.when(sends_at(level) & (z + 1 + i < depth))
            def _():
                sent(zsend, z_send.at[i])


def on_device(mesh_sizes, queries, keys, values, log_decay, gain):
    outer, narrow = mesh_sizes
    tokens, model = queries.shape
    heads = log_decay.shape[0]
    width = model // heads
    depth, rows = split_outer(outer)
    across = narrow // CORES
    chips = rows * across
    per = heads // (chips * CORES)
    groups = heads // per
    levels = max((depth - 1).bit_length(), 1)
    part = width // PARTS
    units = per * PARTS
    lines = -(-per // 8) * 8
    half = lambda *shape: pltpu.VMEM(shape, jnp.bfloat16)
    full = lambda *shape: pltpu.VMEM(shape, jnp.float32)
    dma = lambda *shape: pltpu.SemaphoreType.DMA(shape)
    one = pltpu.SemaphoreType.DMA
    vmem = pl.BlockSpec(memory_space=pltpu.VMEM)
    hbm = pl.BlockSpec(memory_space=pltpu.HBM)
    return pl.pallas_call(
        functools.partial(kernel, (depth, rows, across, heads, width, per)),
        out_shape=jax.ShapeDtypeStruct(queries.shape, jnp.bfloat16),
        in_specs=[hbm] * 5,
        out_specs=vmem,
        scratch_shapes=[
            pltpu.VMEM((tokens, model), queries.dtype),
            pltpu.VMEM((tokens, model), queries.dtype),
            pltpu.VMEM((tokens, model), queries.dtype),
            full(heads, tokens),
            full(1, model),
            full(heads, tokens),
            full(groups, tokens, 128),
            full(groups, tokens, 128),
            full(tokens, tokens),
            full(tokens, model),
            full(heads, tokens, width),
            full(CORES, groups, lines, width),
            full(CORES, chips, lines, width),
            full(chips, lines, width),
            full(chips, lines, width),
            full(chips, lines, width),
            full(depth, lines, width),
            full(levels, lines, width),
            full(lines, width),
            half(per, PARTS, chips, part, width),
            half(CORES, per, PARTS, chips, part, width),
            half(per, PARTS, chips, part, width),
            half(per, PARTS, chips, part, width),
            full(units, part, width),
            half(units, part, width),
            half(levels, units, part, width),
            half(per, PARTS, chips, part, width),
            half(per, PARTS, chips, part, width),
            half(per, PARTS, chips, part, width),
            half(per, PARTS, chips, part, width),
            half(per, PARTS, chips, part, width),
            dma(5),
            one, dma(per), one, one, one, dma(units), one, one,
            dma(max(depth - 1, 1)), dma(depth), dma(max(depth // 2, 1)), dma(levels, units),
            one, dma(units), one, dma(per),
            pltpu.SemaphoreType.REGULAR,
        ],
        compiler_params=pltpu.CompilerParams(
            collective_id=0, has_side_effects=True, vmem_limit_bytes=50 * 1024 * 1024
        ),
    )(queries, keys, values, log_decay, gain.reshape(1, model))


def solution(mesh):
    axes = ("outer", "narrow")
    block = P(axes, None)
    return jax.shard_map(
        functools.partial(on_device, tuple(mesh.shape[a] for a in axes)),
        mesh=mesh,
        in_specs=(block, block, block, P(None, axes), P()),
        out_specs=block,
        check_vma=False,
    )
```

```python
import functools

import jax
import jax.numpy as jnp
from jax import lax
from jax.experimental import pallas as pl
from jax.experimental.pallas import tpu as pltpu
from jax.sharding import PartitionSpec as P

MESH = pl.DeviceIdType.MESH
FAR = -1e30
CORES = 2
PARTS = 2
LAG_Z = 3
LAG_R = 6


def split_outer(outer):
    rows = 1
    for d in range(1, outer + 1):
        if d * d <= outer and outer % d == 0:
            rows = d
    return outer // rows, rows


def kernel(
    sizes, q_hbm, k_hbm, v_hbm, ld_hbm, gain_hbm, out_ref,
    q_ref, k_ref, v_ref, ld_ref, gain_ref, cum, cols_ref, tail_ref, bias, inner, grown,
    tcore, dcore, ptot, tin, dchip, tz, dz, down,
    made, pair, tsend, got_t, q_sum, zsend, got_z, rsend, got_r, own_c, csend, got_c,
    load_sem, kv_sem, made_send, made_recv, ct_send, ct_recv, t_send, t_recv, pt_send, pt_recv,
    zt_send, zt_recv, z_send, z_recv, r_send, r_recv, c_send, c_recv, ready,
):
    depth, rows, across, heads, width, per = sizes
    chips = rows * across
    levels = max(depth - 1, 1).bit_length() if depth > 1 else 0
    tokens = q_ref.shape[0]
    part = width // PARTS
    units = per * PARTS
    unit = 4 if heads % 4 == 0 else 1
    groups = heads // unit
    o, n = lax.axis_index("outer"), lax.axis_index("narrow")
    z, y = o // rows, lax.rem(o, rows)
    x, core = n // CORES, lax.rem(n, CORES)
    me = y * across + x
    first = core == 0

    partner = (o, x * CORES + 1 - core)
    chip_at = lambda p: (z * rows + p // across, lax.rem(p, across) * CORES + core)
    plane_at = lambda j: (j * rows + y, n)
    beside = lambda i: lax.rem(me + i, chips)
    slot = lambda p: lax.rem(p - me - 1 + chips, chips)

    def lanes(h, count=1):
        return pl.ds(pl.multiple_of(h * width, width), count * width)

    span = chips * CORES
    loads = [
        pltpu.make_async_copy(src, dst, load_sem.at[i])
        for i, (src, dst) in enumerate(((ld_hbm, ld_ref), (q_hbm, q_ref), (gain_hbm, gain_ref)))
    ]

    def load_kv(c):
        at = lanes(c * span, span)
        return [
            pltpu.make_async_copy(src.at[:, at], dst.at[:, at], kv_sem.at[c, i])
            for i, (src, dst) in enumerate(((k_hbm, k_ref), (v_hbm, v_ref)))
        ]

    loads[0].start()
    for c in range(per):
        for one in load_kv(c):
            one.start()
    loads[1].start()
    loads[2].start()

    barrier = pltpu.get_barrier_semaphore()
    pl.semaphore_signal(barrier, inc=1, device_id=partner, device_id_type=MESH)
    for i in range(1, chips):
        pl.semaphore_signal(barrier, inc=1, device_id=chip_at(beside(i)), device_id_type=MESH)
    for j in range(1, depth):
        @pl.when(j > z)
        def _():
            pl.semaphore_signal(barrier, inc=1, device_id=plane_at(j), device_id_type=MESH)

    def remote(src, dst, send, recv, where):
        return pltpu.make_async_remote_copy(
            src_ref=src, dst_ref=dst, send_sem=send, recv_sem=recv, device_id=where, device_id_type=MESH
        )

    def arrived(ref, recv):
        remote(ref, ref, made_send, recv, partner).wait_recv()

    def sent(ref, send):
        remote(ref, ref, send, ct_recv, partner).wait_send()

    loads[0].wait()
    total = ld_ref[...]
    lane = lax.broadcasted_iota(jnp.int32, total.shape, 1)
    step = 1
    while step < tokens:
        total = total + jnp.where(lane >= step, pltpu.roll(total, step, axis=1), 0.0)
        step *= 2
    cum[...] = total
    last = jnp.broadcast_to(total[:, tokens - 1 :], (heads, width))
    for c in range(per):
        for g in range(span):
            h = c * span + g
            tcore[core, g, c : c + 1, :] = last[h : h + 1]
    cols = jnp.concatenate([total, jnp.zeros((128 - heads, tokens), jnp.float32)], axis=0).T
    cols_ref[...] = cols
    tail_ref[...] = jnp.exp(cols[tokens - 1 :] - cols)
    at_t = lax.broadcasted_iota(jnp.int32, (width, width), 0)
    at_s = lax.broadcasted_iota(jnp.int32, (width, width), 1)
    bias[...] = jnp.where(at_t >= at_s, 0.0, FAR)

    def states(c, mine):
        a = core if mine else 1 - core
        tails = pltpu.roll(tail_ref[...], lax.rem(128 - (c * span + a), 128), axis=1)
        for p in range(chips):
            at = lanes(c * span + p * CORES + a)
            kept = k_ref[:, at].astype(jnp.float32) * tails[:, p * CORES : p * CORES + 1]
            made_here = lax.dot_general(
                kept.astype(jnp.bfloat16), v_ref[:, at], (((0,), (0,)), ((), ())),
                preferred_element_type=jnp.float32,
            ).astype(jnp.bfloat16)
            for f in range(PARTS):
                piece = made_here[f * part : (f + 1) * part]
                if mine:
                    pair[core, c, f, p] = piece
                else:
                    made[c, f, p] = piece

    def meet(c):
        arrived(pair.at[1 - core, c], made_recv.at[c])
        for f in range(PARTS):
            for p in range(chips):
                decay = dcore[1, p, pl.ds(c, 1), :]
                value = decay * pair[0, c, f, p].astype(jnp.float32) + pair[1, c, f, p].astype(jnp.float32)
                tsend[c, f, slot(p)] = value.astype(jnp.bfloat16)
            for i in range(1, chips):
                remote(
                    tsend.at[c, f, i - 1], got_t.at[c, f, chips - 1 - i], t_send,
                    t_recv.at[c * PARTS + f], chip_at(beside(i)),
                ).start()

    def meet_totals():
        arrived(tcore.at[1 - core], ct_recv)
        for p in range(chips):
            here = [tcore[k, p * CORES + core] for k in range(CORES)]
            for k in range(CORES):
                dcore[k, p] = jnp.exp(here[k])
            ptot[slot(p)] = here[0] + here[1]
        for i in range(1, chips):
            remote(ptot.at[i - 1], tin.at[chips - 1 - i], pt_send, pt_recv, chip_at(beside(i))).start()

    def within(g):
        columns = pltpu.roll(cols_ref[...], lax.rem(128 - g * unit, 128), axis=1)
        for u in range(unit):
            h = g * unit + u
            at = lanes(h)
            column = jnp.broadcast_to(columns[:, u : u + 1], (tokens, width))
            grown[h] = jnp.exp(column)
            row = cum[pl.ds(h, 1), :]
            scores = lax.dot_general(
                q_ref[:, at], k_ref[:, at], (((1,), (1,)), ((), ())),
                preferred_element_type=jnp.float32,
            )
            weights = []
            for t in range(tokens // width):
                rows_t = slice(t * width, (t + 1) * width)
                line = []
                for i in range(tokens // width):
                    at_i = slice(i * width, (i + 1) * width)
                    if i > t:
                        line.append(jnp.zeros((width, width), jnp.bfloat16))
                        continue
                    spread = column[rows_t] - row[:, at_i]
                    if i == t:
                        spread = spread + bias[...]
                    line.append((scores[rows_t, at_i] * jnp.exp(spread)).astype(jnp.bfloat16))
                weights.append(jnp.concatenate(line, axis=1))
            weights = jnp.concatenate(weights, axis=0)
            inner[:, at] = jnp.dot(weights, v_ref[:, at], preferred_element_type=jnp.float32)

    def send_level(level, s):
        for i in range(2**level):
            @pl.when(z + 1 + i < depth)
            def _():
                remote(
                    zsend.at[s], got_z.at[level, s], z_send.at[i], z_recv.at[level, s], plane_at(z + 1 + i)
                ).start()

    def sends_at(level):
        return lax.rem(z, 2 ** (level + 1)) == 2**level - 1

    def plane_totals():
        if chips > 1:
            arrived(tin.at[pl.ds(0, chips - 1)], pt_recv)
        tin[chips - 1] = ptot[chips - 1]
        whole = jnp.zeros_like(tz[0])
        for p in range(chips):
            here = tin[slot(p)]
            dchip[p] = jnp.exp(here)
            whole = whole + here
        tz[z] = whole
        down[...] = jnp.exp(whole)
        if depth > 1:
            @pl.when(z < depth - 1)
            def _():
                pl.semaphore_wait(ready, depth - 1 - z)
            for i in range(1, depth):
                @pl.when(z + i < depth)
                def _():
                    remote(tz.at[z], tz.at[z], zt_send.at[i - 1], zt_recv.at[z], plane_at(z + i)).start()

    def plane(s):
        c, f = s // PARTS, lax.rem(s, PARTS)
        if chips > 1:
            arrived(got_t.at[c, f, pl.ds(0, chips - 1)], t_recv.at[s])
        got_t[c, f, chips - 1] = tsend[c, f, chips - 1]
        acc = got_t[c, f, slot(0)].astype(jnp.float32)
        for p in range(1, chips):
            acc = dchip[p, pl.ds(c, 1), :] * acc + got_t[c, f, slot(p)].astype(jnp.float32)
        q_sum[s] = acc
        if levels:
            @pl.when(sends_at(0))
            def _():
                zsend[s] = acc.astype(jnp.bfloat16)
                send_level(0, s)

    def depth_totals():
        for j in range(depth - 1):
            @pl.when(j < z)
            def _():
                arrived(tz.at[j], zt_recv.at[j])
        for k in range(1, levels):
            start = z // 2**k * 2**k
            whole = jnp.zeros_like(tz[0])
            for j in range(depth - 1):
                whole = whole + jnp.where((j >= start) & (j < z), tz[j], 0.0)
            dz[k] = jnp.exp(whole)

    def scan(s):
        c, f = s // PARTS, lax.rem(s, PARTS)
        acc = jnp.zeros((part, width), jnp.float32)
        for k in range(levels):
            odd = lax.rem(z // 2**k, 2) == 1

            @pl.when(odd)
            def _():
                arrived(got_z.at[k, s], z_recv.at[k, s])

            came = got_z[k, s].astype(jnp.float32)
            if k:
                came = dz[k, pl.ds(c, 1), :] * came + acc
            acc = jnp.where(odd, came, acc)
            if k + 1 < levels:
                @pl.when(sends_at(k + 1))
                def _():
                    zsend[s] = (down[pl.ds(c, 1), :] * acc + q_sum[s]).astype(jnp.bfloat16)
                    send_level(k + 1, s)
        for p in range(chips):
            rsend[c, f, slot(p)] = acc.astype(jnp.bfloat16)
            if p < chips - 1:
                acc = dchip[p, pl.ds(c, 1), :] * acc + got_t[c, f, slot(p)].astype(jnp.float32)
        for i in range(1, chips):
            remote(
                rsend.at[c, f, i - 1], got_r.at[c, f, chips - 1 - i], r_send, r_recv.at[s], chip_at(beside(i))
            ).start()

    def back(s):
        c, f = s // PARTS, lax.rem(s, PARTS)
        if chips > 1:
            arrived(got_r.at[c, f, pl.ds(0, chips - 1)], r_recv.at[s])
        got_r[c, f, chips - 1] = rsend[c, f, chips - 1]
        for p in range(chips):
            before = got_r[c, f, slot(p)]
            after = dcore[0, p, pl.ds(c, 1), :] * before.astype(jnp.float32) + pair[0, c, f, p].astype(jnp.float32)
            after = after.astype(jnp.bfloat16)
            own_c[c, f, p] = jnp.where(first, before, after)
            csend[c, f, p] = jnp.where(first, after, before)
        remote(csend.at[c, f], got_c.at[c, f], c_send, c_recv.at[c], partner).start()

    def finish(c, ref, a):
        for p in range(chips):
            h = c * span + p * CORES + a
            at = lanes(h)
            carried = jnp.concatenate([ref[c, f, p] for f in range(PARTS)], axis=0)
            read = jnp.dot(q_ref[:, at], carried, preferred_element_type=jnp.float32)
            numer = inner[:, at] + read * grown[h]
            mean = jnp.mean(numer * numer, axis=-1, keepdims=True)
            out_ref[:, at] = (numer * lax.rsqrt(mean + 1e-06) * gain_ref[:, at]).astype(jnp.bfloat16)

    def make(c, _):
        for one in load_kv(c):
            one.wait()
        states(c, False)

        @pl.when(c == 0)
        def _():
            pl.semaphore_wait(barrier, chips + z)
            for j in range(depth - 1):
                @pl.when(j < z)
                def _():
                    pl.semaphore_signal(ready, inc=1, device_id=plane_at(j), device_id_type=MESH)
            remote(tcore.at[core], tcore.at[core], ct_send, ct_recv, partner).start()

        remote(made.at[c], pair.at[core, c], made_send, made_recv.at[c], partner).start()

        @pl.when(c > 0)
        def _():
            meet(c - 1)

        states(c, True)

        @pl.when(c == 0)
        def _():
            meet_totals()

        return 0

    lax.fori_loop(0, per, make, 0)
    loads[1].wait()
    loads[2].wait()
    within(0)
    meet(per - 1)
    plane_totals()

    rank = jnp.int32(0)
    for k in range(levels):
        rank = jnp.where(z >= 2**k, k + 1, rank)
    lag_z = jnp.minimum(rank * LAG_Z, units)
    lag_r = lag_z + LAG_R
    lag_f = lag_r + PARTS - 1
    steps = jnp.maximum(lag_f + units, groups - 1)

    def step_at(s, _):
        @pl.when(s < units)
        def _():
            plane(s)

        if levels:
            @pl.when(s == lag_z)
            def _():
                depth_totals()

        @pl.when((s >= lag_z) & (s < lag_z + units))
        def _():
            scan(s - lag_z)

        @pl.when((s >= lag_r) & (s < lag_r + units))
        def _():
            back(s - lag_r)

        t = s - lag_f
        for f in range(PARTS):
            @pl.when((t >= 0) & (lax.rem(t + PARTS, PARTS) == f))
            def _():
                c = t // PARTS
                if f == 0:
                    finish(c, own_c, core)
                if f == PARTS - 1:
                    arrived(got_c.at[c], c_recv.at[c])
                    finish(c, got_c, 1 - core)

        @pl.when(s + 1 < groups)
        def _():
            within(s + 1)

        return 0

    lax.fori_loop(0, steps, step_at, 0)

    sent(made, made_send)
    sent(tcore.at[core], ct_send)
    if chips > 1:
        sent(tsend.at[:, :, pl.ds(0, chips - 1)], t_send)
        sent(ptot.at[pl.ds(0, chips - 1)], pt_send)
        sent(rsend.at[:, :, pl.ds(0, chips - 1)], r_send)
    sent(csend, c_send)
    for i in range(1, depth):
        @pl.when(z + i < depth)
        def _():
            sent(tz.at[z], zt_send.at[i - 1])
    for level in range(levels):
        for i in range(2**level):
            @pl.when(sends_at(level) & (z + 1 + i < depth))
            def _():
                sent(zsend, z_send.at[i])


def on_device(mesh_sizes, queries, keys, values, log_decay, gain):
    outer, narrow = mesh_sizes
    tokens, model = queries.shape
    heads = log_decay.shape[0]
    width = model // heads
    depth, rows = split_outer(outer)
    across = narrow // CORES
    chips = rows * across
    per = heads // (chips * CORES)
    groups = heads // per
    levels = max((depth - 1).bit_length(), 1)
    part = width // PARTS
    units = per * PARTS
    lines = -(-per // 8) * 8
    half = lambda *shape: pltpu.VMEM(shape, jnp.bfloat16)
    full = lambda *shape: pltpu.VMEM(shape, jnp.float32)
    dma = lambda *shape: pltpu.SemaphoreType.DMA(shape)
    one = pltpu.SemaphoreType.DMA
    vmem = pl.BlockSpec(memory_space=pltpu.VMEM)
    hbm = pl.BlockSpec(memory_space=pltpu.HBM)
    arrays = (queries, keys, values, log_decay, gain.reshape(1, model))
    return pl.pallas_call(
        functools.partial(kernel, (depth, rows, across, heads, width, per)),
        out_shape=jax.ShapeDtypeStruct(queries.shape, jnp.bfloat16),
        in_specs=[hbm] * 5,
        out_specs=vmem,
        scratch_shapes=[
            pltpu.VMEM((tokens, model), queries.dtype),
            pltpu.VMEM((tokens, model), queries.dtype),
            pltpu.VMEM((tokens, model), queries.dtype),
            full(heads, tokens),
            full(1, model),
            full(heads, tokens),
            full(tokens, 128),
            full(tokens, 128),
            full(width, width),
            full(tokens, model),
            full(heads, tokens, width),
            full(CORES, groups, lines, width),
            full(CORES, chips, lines, width),
            full(chips, lines, width),
            full(chips, lines, width),
            full(chips, lines, width),
            full(depth, lines, width),
            full(levels, lines, width),
            full(lines, width),
            half(per, PARTS, chips, part, width),
            half(CORES, per, PARTS, chips, part, width),
            half(per, PARTS, chips, part, width),
            half(per, PARTS, chips, part, width),
            full(units, part, width),
            half(units, part, width),
            half(levels, units, part, width),
            half(per, PARTS, chips, part, width),
            half(per, PARTS, chips, part, width),
            half(per, PARTS, chips, part, width),
            half(per, PARTS, chips, part, width),
            half(per, PARTS, chips, part, width),
            dma(3), dma(per, 2),
            one, dma(per), one, one, one, dma(units), one, one,
            dma(max(depth - 1, 1)), dma(depth), dma(max(depth // 2, 1)), dma(levels, units),
            one, dma(units), one, dma(per),
            pltpu.SemaphoreType.REGULAR,
        ],
        compiler_params=pltpu.CompilerParams(
            collective_id=0, has_side_effects=True, vmem_limit_bytes=50 * 1024 * 1024
        ),
    )(*(pltpu.with_memory_space_constraint(a, pltpu.HBM) for a in arrays))


def solution(mesh):
    axes = ("outer", "narrow")
    block = P(axes, None)
    return jax.shard_map(
        functools.partial(on_device, tuple(mesh.shape[a] for a in axes)),
        mesh=mesh,
        in_specs=(block, block, block, P(None, axes), P()),
        out_specs=block,
        check_vma=False,
    )
```

```python
import functools

import jax
import jax.numpy as jnp
from jax import lax
from jax.experimental import pallas as pl
from jax.experimental.pallas import tpu as pltpu
from jax.sharding import PartitionSpec as P

MESH = pl.DeviceIdType.MESH
FAR = -1e30
CORES = 2
PARTS = 2
LAG_Z = 3
LAG_R = 6


def split_outer(outer):
    rows = 1
    for d in range(1, outer + 1):
        if d * d <= outer and outer % d == 0:
            rows = d
    return outer // rows, rows


def kernel(
    sizes, q_hbm, k_hbm, v_hbm, ld_hbm, gain_hbm, out_ref,
    q_ref, k_ref, v_ref, ld_ref, gain_ref, cum, cols_ref, tail_ref, side_ref, bias, inner, grown,
    tcore, dcore, ptot, tin, dchip, tz, dz, down,
    made, pair, tsend, got_t, q_sum, zsend, got_z, rsend, got_r, own_c, csend, got_c,
    load_sem, kv_sem, made_send, made_recv, ct_send, ct_recv, t_send, t_recv, pt_send, pt_recv,
    zt_send, zt_recv, z_send, z_recv, r_send, r_recv, c_send, c_recv, ready,
):
    depth, rows, across, heads, width, per = sizes
    chips = rows * across
    levels = max(depth - 1, 1).bit_length() if depth > 1 else 0
    tokens = q_ref.shape[0]
    part = width // PARTS
    units = per * PARTS
    unit = 4 if heads % 4 == 0 else 1
    groups = heads // unit
    o, n = lax.axis_index("outer"), lax.axis_index("narrow")
    z, y = o // rows, lax.rem(o, rows)
    x, core = n // CORES, lax.rem(n, CORES)
    me = y * across + x
    first = core == 0

    partner = (o, x * CORES + 1 - core)
    chip_at = lambda p: (z * rows + p // across, lax.rem(p, across) * CORES + core)
    plane_at = lambda j: (j * rows + y, n)
    beside = lambda i: lax.rem(me + i, chips)
    slot = lambda p: lax.rem(p - me - 1 + chips, chips)

    def lanes(h, count=1):
        return pl.ds(pl.multiple_of(h * width, width), count * width)

    span = chips * CORES
    loads = [
        pltpu.make_async_copy(src, dst, load_sem.at[i])
        for i, (src, dst) in enumerate(((ld_hbm, ld_ref), (q_hbm, q_ref), (gain_hbm, gain_ref)))
    ]

    def load_kv(c):
        at = lanes(c * span, span)
        return [
            pltpu.make_async_copy(src.at[:, at], dst.at[:, at], kv_sem.at[c, i])
            for i, (src, dst) in enumerate(((k_hbm, k_ref), (v_hbm, v_ref)))
        ]

    loads[0].start()
    for one in load_kv(0):
        one.start()

    barrier = pltpu.get_barrier_semaphore()
    pl.semaphore_signal(barrier, inc=1, device_id=partner, device_id_type=MESH)
    for i in range(1, chips):
        pl.semaphore_signal(barrier, inc=1, device_id=chip_at(beside(i)), device_id_type=MESH)
    for j in range(1, depth):
        @pl.when(j > z)
        def _():
            pl.semaphore_signal(barrier, inc=1, device_id=plane_at(j), device_id_type=MESH)

    def remote(src, dst, send, recv, where):
        return pltpu.make_async_remote_copy(
            src_ref=src, dst_ref=dst, send_sem=send, recv_sem=recv, device_id=where, device_id_type=MESH
        )

    def arrived(ref, recv):
        remote(ref, ref, made_send, recv, partner).wait_recv()

    def sent(ref, send):
        remote(ref, ref, send, ct_recv, partner).wait_send()

    loads[0].wait()
    for c in range(1, per):
        for one in load_kv(c):
            one.start()
    loads[1].start()
    loads[2].start()
    total = ld_ref[...]
    lane = lax.broadcasted_iota(jnp.int32, total.shape, 1)
    step = 1
    while step < tokens:
        total = total + jnp.where(lane >= step, pltpu.roll(total, step, axis=1), 0.0)
        step *= 2
    cum[...] = total
    last = jnp.broadcast_to(total[:, tokens - 1 :], (heads, width))
    for c in range(per):
        for g in range(span):
            h = c * span + g
            tcore[core, g, c : c + 1, :] = last[h : h + 1]
    cols = jnp.concatenate([total, jnp.zeros((128 - heads, tokens), jnp.float32)], axis=0).T
    cols_ref[...] = cols
    tail = jnp.exp(cols[tokens - 1 :] - cols)
    tail_ref[...] = pltpu.roll(tail, lax.rem(128 - core, 128), axis=1)
    side_ref[...] = pltpu.roll(tail, 127 + core, axis=1)
    at_t = lax.broadcasted_iota(jnp.int32, (width, width), 0)
    at_s = lax.broadcasted_iota(jnp.int32, (width, width), 1)
    bias[...] = jnp.where(at_t >= at_s, 0.0, FAR)

    def states(c, mine):
        a = core if mine else 1 - core
        tails = tail_ref if mine else side_ref
        for p in range(chips):
            u = c * span + p * CORES
            at = lanes(c * span + p * CORES + a)
            kept = k_ref[:, at].astype(jnp.float32) * tails[:, u : u + 1]
            made_here = lax.dot_general(
                kept.astype(jnp.bfloat16), v_ref[:, at], (((0,), (0,)), ((), ())),
                preferred_element_type=jnp.float32,
            ).astype(jnp.bfloat16)
            for f in range(PARTS):
                piece = made_here[f * part : (f + 1) * part]
                if mine:
                    pair[core, c, f, p] = piece
                else:
                    made[c, f, p] = piece

    def meet(c):
        arrived(pair.at[1 - core, c], made_recv.at[c])
        for f in range(PARTS):
            for p in range(chips):
                decay = dcore[1, p, pl.ds(c, 1), :]
                value = decay * pair[0, c, f, p].astype(jnp.float32) + pair[1, c, f, p].astype(jnp.float32)
                tsend[c, f, slot(p)] = value.astype(jnp.bfloat16)
            for i in range(1, chips):
                remote(
                    tsend.at[c, f, i - 1], got_t.at[c, f, chips - 1 - i], t_send,
                    t_recv.at[c * PARTS + f], chip_at(beside(i)),
                ).start()

    def meet_totals():
        arrived(tcore.at[1 - core], ct_recv)
        for p in range(chips):
            here = [tcore[k, p * CORES + core] for k in range(CORES)]
            for k in range(CORES):
                dcore[k, p] = jnp.exp(here[k])
            ptot[slot(p)] = here[0] + here[1]
        for i in range(1, chips):
            remote(ptot.at[i - 1], tin.at[chips - 1 - i], pt_send, pt_recv, chip_at(beside(i))).start()

    def within(g):
        for h in range(g * unit, (g + 1) * unit):
            at = slice(h * width, (h + 1) * width)
            column = jnp.broadcast_to(cols_ref[:, h : h + 1], (tokens, width))
            grown[h] = jnp.exp(column)
            row = cum[h : h + 1, :]
            scores = lax.dot_general(
                q_ref[:, at], k_ref[:, at], (((1,), (1,)), ((), ())),
                preferred_element_type=jnp.float32,
            )
            weights = []
            for t in range(tokens // width):
                rows_t = slice(t * width, (t + 1) * width)
                line = []
                for i in range(tokens // width):
                    at_i = slice(i * width, (i + 1) * width)
                    if i > t:
                        line.append(jnp.zeros((width, width), jnp.bfloat16))
                        continue
                    spread = column[rows_t] - row[:, at_i]
                    if i == t:
                        spread = spread + bias[...]
                    line.append((scores[rows_t, at_i] * jnp.exp(spread)).astype(jnp.bfloat16))
                weights.append(jnp.concatenate(line, axis=1))
            weights = jnp.concatenate(weights, axis=0)
            inner[:, at] = jnp.dot(weights, v_ref[:, at], preferred_element_type=jnp.float32)

    def send_level(level, s):
        for i in range(2**level):
            @pl.when(z + 1 + i < depth)
            def _():
                remote(
                    zsend.at[s], got_z.at[level, s], z_send.at[i], z_recv.at[level, s], plane_at(z + 1 + i)
                ).start()

    def sends_at(level):
        return lax.rem(z, 2 ** (level + 1)) == 2**level - 1

    def plane_totals():
        if chips > 1:
            arrived(tin.at[pl.ds(0, chips - 1)], pt_recv)
        tin[chips - 1] = ptot[chips - 1]
        whole = jnp.zeros_like(tz[0])
        for p in range(chips):
            here = tin[slot(p)]
            dchip[p] = jnp.exp(here)
            whole = whole + here
        tz[z] = whole
        down[...] = jnp.exp(whole)
        if depth > 1:
            @pl.when(z < depth - 1)
            def _():
                pl.semaphore_wait(ready, depth - 1 - z)
            for i in range(1, depth):
                @pl.when(z + i < depth)
                def _():
                    remote(tz.at[z], tz.at[z], zt_send.at[i - 1], zt_recv.at[z], plane_at(z + i)).start()

    def plane(s):
        c, f = s // PARTS, lax.rem(s, PARTS)
        if chips > 1:
            arrived(got_t.at[c, f, pl.ds(0, chips - 1)], t_recv.at[s])
        got_t[c, f, chips - 1] = tsend[c, f, chips - 1]
        acc = got_t[c, f, slot(0)].astype(jnp.float32)
        for p in range(1, chips):
            acc = dchip[p, pl.ds(c, 1), :] * acc + got_t[c, f, slot(p)].astype(jnp.float32)
        q_sum[s] = acc
        if levels:
            @pl.when(sends_at(0))
            def _():
                zsend[s] = acc.astype(jnp.bfloat16)
                send_level(0, s)

    def depth_totals():
        for j in range(depth - 1):
            @pl.when(j < z)
            def _():
                arrived(tz.at[j], zt_recv.at[j])
        for k in range(1, levels):
            start = z // 2**k * 2**k
            whole = jnp.zeros_like(tz[0])
            for j in range(depth - 1):
                whole = whole + jnp.where((j >= start) & (j < z), tz[j], 0.0)
            dz[k] = jnp.exp(whole)

    def scan(s):
        c, f = s // PARTS, lax.rem(s, PARTS)
        acc = jnp.zeros((part, width), jnp.float32)
        for k in range(levels):
            odd = lax.rem(z // 2**k, 2) == 1

            @pl.when(odd)
            def _():
                arrived(got_z.at[k, s], z_recv.at[k, s])

            came = got_z[k, s].astype(jnp.float32)
            if k:
                came = dz[k, pl.ds(c, 1), :] * came + acc
            acc = jnp.where(odd, came, acc)
            if k + 1 < levels:
                @pl.when(sends_at(k + 1))
                def _():
                    zsend[s] = (down[pl.ds(c, 1), :] * acc + q_sum[s]).astype(jnp.bfloat16)
                    send_level(k + 1, s)
        for p in range(chips):
            rsend[c, f, slot(p)] = acc.astype(jnp.bfloat16)
            if p < chips - 1:
                acc = dchip[p, pl.ds(c, 1), :] * acc + got_t[c, f, slot(p)].astype(jnp.float32)
        for i in range(1, chips):
            remote(
                rsend.at[c, f, i - 1], got_r.at[c, f, chips - 1 - i], r_send, r_recv.at[s], chip_at(beside(i))
            ).start()

    def back(s):
        c, f = s // PARTS, lax.rem(s, PARTS)
        if chips > 1:
            arrived(got_r.at[c, f, pl.ds(0, chips - 1)], r_recv.at[s])
        got_r[c, f, chips - 1] = rsend[c, f, chips - 1]
        for p in range(chips):
            before = got_r[c, f, slot(p)]
            after = dcore[0, p, pl.ds(c, 1), :] * before.astype(jnp.float32) + pair[0, c, f, p].astype(jnp.float32)
            after = after.astype(jnp.bfloat16)
            own_c[c, f, p] = jnp.where(first, before, after)
            csend[c, f, p] = jnp.where(first, after, before)
        remote(csend.at[c, f], got_c.at[c, f], c_send, c_recv.at[c], partner).start()

    def finish(c, ref, a):
        for p in range(chips):
            h = c * span + p * CORES + a
            at = lanes(h)
            carried = jnp.concatenate([ref[c, f, p] for f in range(PARTS)], axis=0)
            read = jnp.dot(q_ref[:, at], carried, preferred_element_type=jnp.float32)
            numer = inner[:, at] + read * grown[h]
            mean = jnp.mean(numer * numer, axis=-1, keepdims=True)
            out_ref[:, at] = (numer * lax.rsqrt(mean + 1e-06) * gain_ref[:, at]).astype(jnp.bfloat16)

    for c in range(per):
        for one in load_kv(c):
            one.wait()
        states(c, False)
        if c == 0:
            pl.semaphore_wait(barrier, chips + z)
            for j in range(depth - 1):
                @pl.when(j < z)
                def _():
                    pl.semaphore_signal(ready, inc=1, device_id=plane_at(j), device_id_type=MESH)
            remote(tcore.at[core], tcore.at[core], ct_send, ct_recv, partner).start()
        remote(made.at[c], pair.at[core, c], made_send, made_recv.at[c], partner).start()
        if c:
            meet(c - 1)
        states(c, True)
        if c == 0:
            meet_totals()
    loads[1].wait()
    loads[2].wait()
    within(0)
    meet(per - 1)
    plane_totals()

    slots = [g + g // 3 for g in range(groups - 1)]

    rank = jnp.int32(0)
    for k in range(levels):
        rank = jnp.where(z >= 2**k, k + 1, rank)
    lag_z = jnp.minimum(rank * LAG_Z, units)
    lag_r = lag_z + jnp.where(rank == levels, min(LAG_R, units), units)
    lag_f = lag_r + PARTS - 1
    steps = jnp.maximum(lag_f + units + 2, max(slots, default=0) + 1)

    def step_at(s, _):
        @pl.when(s < units)
        def _():
            plane(s)

        if levels:
            @pl.when(s == lag_z)
            def _():
                depth_totals()

        @pl.when((s >= lag_z) & (s < lag_z + units))
        def _():
            scan(s - lag_z)

        @pl.when((s >= lag_r) & (s < lag_r + units))
        def _():
            back(s - lag_r)

        t = s - lag_f

        @pl.when((t >= 0) & (t < units) & (lax.rem(t + units, PARTS) == 0))
        def _():
            finish(t // PARTS, own_c, core)

        t = t - PARTS - 1

        @pl.when((t >= 0) & (lax.rem(t + units, PARTS) == 0))
        def _():
            arrived(got_c.at[t // PARTS], c_recv.at[t // PARTS])
            finish(t // PARTS, got_c, 1 - core)

        for g in range(1, groups):
            @pl.when(s == slots[g - 1])
            def _():
                within(g)

        return 0

    lax.fori_loop(0, steps, step_at, 0)

    sent(made, made_send)
    sent(tcore.at[core], ct_send)
    if chips > 1:
        sent(tsend.at[:, :, pl.ds(0, chips - 1)], t_send)
        sent(ptot.at[pl.ds(0, chips - 1)], pt_send)
        sent(rsend.at[:, :, pl.ds(0, chips - 1)], r_send)
    sent(csend, c_send)
    for i in range(1, depth):
        @pl.when(z + i < depth)
        def _():
            sent(tz.at[z], zt_send.at[i - 1])
    for level in range(levels):
        for i in range(2**level):
            @pl.when(sends_at(level) & (z + 1 + i < depth))
            def _():
                sent(zsend, z_send.at[i])


def on_device(mesh_sizes, queries, keys, values, log_decay, gain):
    outer, narrow = mesh_sizes
    tokens, model = queries.shape
    heads = log_decay.shape[0]
    width = model // heads
    depth, rows = split_outer(outer)
    across = narrow // CORES
    chips = rows * across
    per = heads // (chips * CORES)
    groups = heads // per
    levels = max((depth - 1).bit_length(), 1)
    part = width // PARTS
    units = per * PARTS
    lines = -(-per // 8) * 8
    half = lambda *shape: pltpu.VMEM(shape, jnp.bfloat16)
    full = lambda *shape: pltpu.VMEM(shape, jnp.float32)
    dma = lambda *shape: pltpu.SemaphoreType.DMA(shape)
    one = pltpu.SemaphoreType.DMA
    vmem = pl.BlockSpec(memory_space=pltpu.VMEM)
    hbm = pl.BlockSpec(memory_space=pltpu.HBM)
    arrays = (queries, keys, values, log_decay, gain.reshape(1, model))
    return pl.pallas_call(
        functools.partial(kernel, (depth, rows, across, heads, width, per)),
        out_shape=jax.ShapeDtypeStruct(queries.shape, jnp.bfloat16),
        in_specs=[hbm] * 5,
        out_specs=vmem,
        scratch_shapes=[
            pltpu.VMEM((tokens, model), queries.dtype),
            pltpu.VMEM((tokens, model), queries.dtype),
            pltpu.VMEM((tokens, model), queries.dtype),
            full(heads, tokens),
            full(1, model),
            full(heads, tokens),
            full(tokens, 128),
            full(tokens, 128),
            full(tokens, 128),
            full(width, width),
            full(tokens, model),
            full(heads, tokens, width),
            full(CORES, groups, lines, width),
            full(CORES, chips, lines, width),
            full(chips, lines, width),
            full(chips, lines, width),
            full(chips, lines, width),
            full(depth, lines, width),
            full(levels, lines, width),
            full(lines, width),
            half(per, PARTS, chips, part, width),
            half(CORES, per, PARTS, chips, part, width),
            half(per, PARTS, chips, part, width),
            half(per, PARTS, chips, part, width),
            full(units, part, width),
            half(units, part, width),
            half(levels, units, part, width),
            half(per, PARTS, chips, part, width),
            half(per, PARTS, chips, part, width),
            half(per, PARTS, chips, part, width),
            half(per, PARTS, chips, part, width),
            half(per, PARTS, chips, part, width),
            dma(3), dma(per, 2),
            one, dma(per), one, one, one, dma(units), one, one,
            dma(max(depth - 1, 1)), dma(depth), dma(max(depth // 2, 1)), dma(levels, units),
            one, dma(units), one, dma(per),
            pltpu.SemaphoreType.REGULAR,
        ],
        compiler_params=pltpu.CompilerParams(
            collective_id=0, has_side_effects=True, vmem_limit_bytes=50 * 1024 * 1024
        ),
    )(*(pltpu.with_memory_space_constraint(a, pltpu.HBM) for a in arrays))


def solution(mesh):
    axes = ("outer", "narrow")
    block = P(axes, None)
    return jax.shard_map(
        functools.partial(on_device, tuple(mesh.shape[a] for a in axes)),
        mesh=mesh,
        in_specs=(block, block, block, P(None, axes), P()),
        out_specs=block,
        check_vma=False,
    )
```

```python
import functools

import jax
import jax.numpy as jnp
from jax import lax
from jax.experimental import pallas as pl
from jax.experimental.pallas import tpu as pltpu
from jax.sharding import PartitionSpec as P

MESH = pl.DeviceIdType.MESH
FAR = -1e30
CORES = 2
PARTS = 2
LAG_Z = 2
LAG_R = 6
BUSY = 3


def split_outer(outer):
    rows = 1
    for d in range(1, outer + 1):
        if d * d <= outer and outer % d == 0:
            rows = d
    return outer // rows, rows


def kernel(
    sizes, q_hbm, k_hbm, v_hbm, ld_hbm, gain_hbm, out_ref,
    q_ref, k_ref, v_ref, ld_ref, gain_ref, cum, cols_ref, grow_ref, tail_ref, side_ref, bias, inner, grown,
    tcore, dcore, ptot, tin, dchip, tz, dz, down,
    made, pair, tsend, got_t, q_sum, zsend, got_z, rsend, got_r, own_c, csend, got_c,
    load_sem, kv_sem, made_send, made_recv, ct_send, ct_recv, t_send, t_recv, pt_send, pt_recv,
    zt_send, zt_recv, z_send, z_recv, r_send, r_recv, c_send, c_recv, ready,
):
    depth, rows, across, heads, width, per = sizes
    chips = rows * across
    levels = max(depth - 1, 1).bit_length() if depth > 1 else 0
    tokens = q_ref.shape[0]
    part = width // PARTS
    units = per * PARTS
    unit = 4 if heads % 4 == 0 else 1
    groups = heads // unit
    o, n = lax.axis_index("outer"), lax.axis_index("narrow")
    z, y = o // rows, lax.rem(o, rows)
    x, core = n // CORES, lax.rem(n, CORES)
    me = y * across + x
    first = core == 0

    partner = (o, x * CORES + 1 - core)
    chip_at = lambda p: (z * rows + p // across, lax.rem(p, across) * CORES + core)
    plane_at = lambda j: (j * rows + y, n)
    beside = lambda i: lax.rem(y + i // across, rows) * across + lax.rem(x + i % across, across)
    back_slot = lambda i: (-(i // across) % rows) * across + -i % across - 1
    served = sorted(range(1, chips), key=lambda i: (-(i // across > 0) - (i % across > 0), i))

    def slot(p):
        i = lax.rem(p // across - y + rows, rows) * across + lax.rem(p % across - x + across, across)
        return lax.rem(i - 1 + chips, chips)


    def lanes(h, count=1):
        return pl.ds(pl.multiple_of(h * width, width), count * width)

    span = chips * CORES
    loads = [
        pltpu.make_async_copy(src, dst, load_sem.at[i])
        for i, (src, dst) in enumerate(((ld_hbm, ld_ref), (q_hbm, q_ref), (gain_hbm, gain_ref)))
    ]

    def load_kv(c):
        at = lanes(c * span, span)
        return [
            pltpu.make_async_copy(src.at[:, at], dst.at[:, at], kv_sem.at[c, i])
            for i, (src, dst) in enumerate(((k_hbm, k_ref), (v_hbm, v_ref)))
        ]

    loads[0].start()
    for one in load_kv(0):
        one.start()

    barrier = pltpu.get_barrier_semaphore()
    pl.semaphore_signal(barrier, inc=1, device_id=partner, device_id_type=MESH)
    for i in range(1, chips):
        pl.semaphore_signal(barrier, inc=1, device_id=chip_at(beside(i)), device_id_type=MESH)
    for j in range(1, depth):
        @pl.when(j > z)
        def _():
            pl.semaphore_signal(barrier, inc=1, device_id=plane_at(j), device_id_type=MESH)

    def remote(src, dst, send, recv, where):
        return pltpu.make_async_remote_copy(
            src_ref=src, dst_ref=dst, send_sem=send, recv_sem=recv, device_id=where, device_id_type=MESH
        )

    def arrived(ref, recv):
        remote(ref, ref, made_send, recv, partner).wait_recv()

    def sent(ref, send):
        remote(ref, ref, send, ct_recv, partner).wait_send()

    loads[0].wait()
    cols = jnp.concatenate([ld_ref[...], jnp.zeros((128 - heads, tokens), jnp.float32)], axis=0).T
    line = lax.broadcasted_iota(jnp.int32, cols.shape, 0)
    step = 1
    while step < tokens:
        if step < 8:
            moved = jnp.where(line >= step, pltpu.roll(cols, step, axis=0), 0.0)
        else:
            moved = jnp.concatenate([jnp.zeros((step, 128), jnp.float32), cols[: tokens - step]], axis=0)
        cols = cols + moved
        step *= 2
    cols_ref[...] = cols
    tail = jnp.exp(cols[tokens - 1 :] - cols)
    side_ref[...] = pltpu.roll(tail, 127 + core, axis=1)
    tail_ref[...] = pltpu.roll(tail, lax.rem(128 - core, 128), axis=1)
    for c in range(1, per):
        for one in load_kv(c):
            one.start()
    loads[1].start()
    loads[2].start()

    def decay_rows():
        grow_ref[...] = jnp.exp(cols_ref[...])
        total = cols_ref[...].T[:heads]
        cum[...] = total
        last = jnp.broadcast_to(total[:, tokens - 1 :], (heads, width))
        for c in range(per):
            for g in range(span):
                h = c * span + g
                tcore[core, g, c : c + 1, :] = last[h : h + 1]
        remote(tcore.at[core], tcore.at[core], ct_send, ct_recv, partner).start()
        at_t = lax.broadcasted_iota(jnp.int32, (width, width), 0)
        at_s = lax.broadcasted_iota(jnp.int32, (width, width), 1)
        bias[...] = jnp.where(at_t >= at_s, 0.0, FAR)

    def states(c, mine, some=None):
        a = core if mine else 1 - core
        tails = tail_ref if mine else side_ref
        for p in some or range(chips):
            u = c * span + p * CORES
            at = lanes(c * span + p * CORES + a)
            kept = k_ref[:, at].astype(jnp.float32) * tails[:, u : u + 1]
            made_here = lax.dot_general(
                kept.astype(jnp.bfloat16), v_ref[:, at], (((0,), (0,)), ((), ())),
                preferred_element_type=jnp.float32,
            ).astype(jnp.bfloat16)
            for f in range(PARTS):
                piece = made_here[f * part : (f + 1) * part]
                if mine:
                    pair[core, c, f, p] = piece
                else:
                    made[c, f, p] = piece

    def meet(c):
        arrived(pair.at[1 - core, c], made_recv.at[c])
        for f in range(PARTS):
            for p in range(chips):
                decay = dcore[1, p, pl.ds(c, 1), :]
                value = decay * pair[0, c, f, p].astype(jnp.float32) + pair[1, c, f, p].astype(jnp.float32)
                tsend[c, f, slot(p)] = value.astype(jnp.bfloat16)
            for i in served:
                remote(
                    tsend.at[c, f, i - 1], got_t.at[c, f, back_slot(i)], t_send,
                    t_recv.at[c * PARTS + f], chip_at(beside(i)),
                ).start()

    def meet_totals():
        arrived(tcore.at[1 - core], ct_recv)
        for p in range(chips):
            here = [tcore[k, p * CORES + core] for k in range(CORES)]
            for k in range(CORES):
                dcore[k, p] = jnp.exp(here[k])
            ptot[slot(p)] = here[0] + here[1]
        for i in range(1, chips):
            remote(ptot.at[i - 1], tin.at[back_slot(i)], pt_send, pt_recv, chip_at(beside(i))).start()

    def within(g):
        for h in range(g * unit, (g + 1) * unit):
            at = slice(h * width, (h + 1) * width)
            column = jnp.broadcast_to(cols_ref[:, h : h + 1], (tokens, width))
            grown[h] = jnp.broadcast_to(grow_ref[:, h : h + 1], (tokens, width))
            row = cum[h : h + 1, :]
            scores = lax.dot_general(
                q_ref[:, at], k_ref[:, at], (((1,), (1,)), ((), ())),
                preferred_element_type=jnp.float32,
            )
            weights = []
            for t in range(tokens // width):
                rows_t = slice(t * width, (t + 1) * width)
                line = []
                for i in range(tokens // width):
                    at_i = slice(i * width, (i + 1) * width)
                    if i > t:
                        line.append(jnp.zeros((width, width), jnp.bfloat16))
                        continue
                    spread = column[rows_t] - row[:, at_i]
                    if i == t:
                        spread = spread + bias[...]
                    line.append((scores[rows_t, at_i] * jnp.exp(spread)).astype(jnp.bfloat16))
                weights.append(jnp.concatenate(line, axis=1))
            weights = jnp.concatenate(weights, axis=0)
            inner[:, at] = jnp.dot(weights, v_ref[:, at], preferred_element_type=jnp.float32)

    def send_level(level, s):
        for i in range(2**level):
            @pl.when(z + 1 + i < depth)
            def _():
                remote(
                    zsend.at[s], got_z.at[level, s], z_send.at[i], z_recv.at[level, s], plane_at(z + 1 + i)
                ).start()

    def sends_at(level):
        return lax.rem(z, 2 ** (level + 1)) == 2**level - 1

    def plane_totals():
        if chips > 1:
            arrived(tin.at[pl.ds(0, chips - 1)], pt_recv)
        tin[chips - 1] = ptot[chips - 1]
        whole = jnp.zeros_like(tz[0])
        for p in range(chips):
            here = tin[slot(p)]
            dchip[p] = jnp.exp(here)
            whole = whole + here
        tz[z] = whole
        down[...] = jnp.exp(whole)
        if depth > 1:
            @pl.when(z < depth - 1)
            def _():
                pl.semaphore_wait(ready, depth - 1 - z)
            for i in range(1, depth):
                @pl.when(z + i < depth)
                def _():
                    remote(tz.at[z], tz.at[z], zt_send.at[i - 1], zt_recv.at[z], plane_at(z + i)).start()

    def plane(s):
        c, f = s // PARTS, lax.rem(s, PARTS)
        if chips > 1:
            arrived(got_t.at[c, f, pl.ds(0, chips - 1)], t_recv.at[s])
        got_t[c, f, chips - 1] = tsend[c, f, chips - 1]
        acc = got_t[c, f, slot(0)].astype(jnp.float32)
        for p in range(1, chips):
            acc = dchip[p, pl.ds(c, 1), :] * acc + got_t[c, f, slot(p)].astype(jnp.float32)
        q_sum[s] = acc
        if levels:
            @pl.when(sends_at(0))
            def _():
                zsend[s] = acc.astype(jnp.bfloat16)
                send_level(0, s)

    def depth_totals():
        for j in range(depth - 1):
            @pl.when(j < z)
            def _():
                arrived(tz.at[j], zt_recv.at[j])
        for k in range(1, levels):
            start = z // 2**k * 2**k
            whole = jnp.zeros_like(tz[0])
            for j in range(depth - 1):
                whole = whole + jnp.where((j >= start) & (j < z), tz[j], 0.0)
            dz[k] = jnp.exp(whole)

    def scan(s):
        c, f = s // PARTS, lax.rem(s, PARTS)
        acc = jnp.zeros((part, width), jnp.float32)
        for k in range(levels):
            odd = lax.rem(z // 2**k, 2) == 1

            @pl.when(odd)
            def _():
                arrived(got_z.at[k, s], z_recv.at[k, s])

            came = got_z[k, s].astype(jnp.float32)
            if k:
                came = dz[k, pl.ds(c, 1), :] * came + acc
            acc = jnp.where(odd, came, acc)
            if k + 1 < levels:
                @pl.when(sends_at(k + 1))
                def _():
                    zsend[s] = (down[pl.ds(c, 1), :] * acc + q_sum[s]).astype(jnp.bfloat16)
                    send_level(k + 1, s)
        for p in range(chips):
            rsend[c, f, slot(p)] = acc.astype(jnp.bfloat16)
            if p < chips - 1:
                acc = dchip[p, pl.ds(c, 1), :] * acc + got_t[c, f, slot(p)].astype(jnp.float32)
        for i in served:
            remote(
                rsend.at[c, f, i - 1], got_r.at[c, f, back_slot(i)], r_send, r_recv.at[s], chip_at(beside(i))
            ).start()

    def back(s):
        c, f = s // PARTS, lax.rem(s, PARTS)
        if chips > 1:
            arrived(got_r.at[c, f, pl.ds(0, chips - 1)], r_recv.at[s])
        got_r[c, f, chips - 1] = rsend[c, f, chips - 1]
        for p in range(chips):
            before = got_r[c, f, slot(p)]
            after = dcore[0, p, pl.ds(c, 1), :] * before.astype(jnp.float32) + pair[0, c, f, p].astype(jnp.float32)
            after = after.astype(jnp.bfloat16)
            own_c[c, f, p] = jnp.where(first, before, after)
            csend[c, f, p] = jnp.where(first, after, before)
        remote(csend.at[c, f], got_c.at[c, f], c_send, c_recv.at[c], partner).start()

    def finish(c, ref, a):
        for p in range(chips):
            h = c * span + p * CORES + a
            at = lanes(h)
            carried = jnp.concatenate([ref[c, f, p] for f in range(PARTS)], axis=0)
            read = jnp.dot(q_ref[:, at], carried, preferred_element_type=jnp.float32)
            numer = inner[:, at] + read * grown[h]
            mean = jnp.mean(numer * numer, axis=-1, keepdims=True)
            out_ref[:, at] = (numer * lax.rsqrt(mean + 1e-06) * gain_ref[:, at]).astype(jnp.bfloat16)

    for c in range(per):
        if c != 1:
            for one in load_kv(c):
                one.wait()
        states(c, False, range(chips // 2 if c == 1 else 0, chips))
        if c == 0:
            pl.semaphore_wait(barrier, chips + z)
            for j in range(depth - 1):
                @pl.when(j < z)
                def _():
                    pl.semaphore_signal(ready, inc=1, device_id=plane_at(j), device_id_type=MESH)
        remote(made.at[c], pair.at[core, c], made_send, made_recv.at[c], partner).start()
        if c == 0:
            decay_rows()
        if c > 1:
            meet(c - 1)
        states(c, True)
        if c == 0 and per > 1:
            for one in load_kv(1):
                one.wait()
            states(1, False, range(chips // 2))
            meet_totals()
            meet(0)
    if per == 1:
        meet_totals()
    loads[1].wait()
    loads[2].wait()
    within(0)
    meet(per - 1)
    plane_totals()


    rank = jnp.int32(0)
    for k in range(levels):
        rank = jnp.where(z >= 2**k, k + 1, rank)
    lag_z = jnp.minimum(jnp.where(rank == levels, units, jnp.where(rank == 0, 2 * LAG_Z, LAG_Z)), units)
    lag_r = lag_z + jnp.where(rank == levels, min(LAG_R, units), units)
    inner_planes = rank == levels
    slots = [jnp.where(inner_planes, g + g // 3, g if g < BUSY else max(g, units + LAG_Z + g - BUSY)) for g in range(groups - 1)]
    steps = jnp.maximum(lag_r + units + 2, units + LAG_Z + groups)

    def step_at(s, _):
        @pl.when(s < units)
        def _():
            plane(s)

        if levels:
            @pl.when(s == lag_z)
            def _():
                depth_totals()

        @pl.when((s >= lag_z) & (s < lag_z + units))
        def _():
            scan(s - lag_z)

        @pl.when((s >= lag_r) & (s < lag_r + units))
        def _():
            back(s - lag_r)

        t = s - lag_r

        @pl.when((t >= 0) & (t < units) & (lax.rem(t + units, PARTS) == PARTS - 1))
        def _():
            finish(t // PARTS, own_c, core)

        end = t == units + 1
        c = jnp.where(end, per - 1, (t - 2 * PARTS) // PARTS)

        @pl.when(end | ((t >= 2 * PARTS) & (t <= units) & (lax.rem(t + units, PARTS) == 0)))
        def _():
            arrived(got_c.at[c], c_recv.at[c])
            finish(c, got_c, 1 - core)

        for g in range(1, groups):
            @pl.when(s == slots[g - 1])
            def _():
                within(g)

        return 0

    lax.fori_loop(0, steps, step_at, 0)

    sent(made, made_send)
    sent(tcore.at[core], ct_send)
    if chips > 1:
        sent(tsend.at[:, :, pl.ds(0, chips - 1)], t_send)
        sent(ptot.at[pl.ds(0, chips - 1)], pt_send)
        sent(rsend.at[:, :, pl.ds(0, chips - 1)], r_send)
    sent(csend, c_send)
    for i in range(1, depth):
        @pl.when(z + i < depth)
        def _():
            sent(tz.at[z], zt_send.at[i - 1])
    for level in range(levels):
        for i in range(2**level):
            @pl.when(sends_at(level) & (z + 1 + i < depth))
            def _():
                sent(zsend, z_send.at[i])


def on_device(mesh_sizes, queries, keys, values, log_decay, gain):
    outer, narrow = mesh_sizes
    tokens, model = queries.shape
    heads = log_decay.shape[0]
    width = model // heads
    depth, rows = split_outer(outer)
    across = narrow // CORES
    chips = rows * across
    per = heads // (chips * CORES)
    groups = heads // per
    levels = max((depth - 1).bit_length(), 1)
    part = width // PARTS
    units = per * PARTS
    lines = -(-per // 8) * 8
    half = lambda *shape: pltpu.VMEM(shape, jnp.bfloat16)
    full = lambda *shape: pltpu.VMEM(shape, jnp.float32)
    dma = lambda *shape: pltpu.SemaphoreType.DMA(shape)
    one = pltpu.SemaphoreType.DMA
    vmem = pl.BlockSpec(memory_space=pltpu.VMEM)
    hbm = pl.BlockSpec(memory_space=pltpu.HBM)
    arrays = (queries, keys, values, log_decay, gain.reshape(1, model))
    return pl.pallas_call(
        functools.partial(kernel, (depth, rows, across, heads, width, per)),
        out_shape=jax.ShapeDtypeStruct(queries.shape, jnp.bfloat16),
        in_specs=[hbm] * 5,
        out_specs=vmem,
        scratch_shapes=[
            pltpu.VMEM((tokens, model), queries.dtype),
            pltpu.VMEM((tokens, model), queries.dtype),
            pltpu.VMEM((tokens, model), queries.dtype),
            full(heads, tokens),
            full(1, model),
            full(heads, tokens),
            full(tokens, 128),
            full(tokens, 128),
            full(tokens, 128),
            full(tokens, 128),
            full(width, width),
            full(tokens, model),
            full(heads, tokens, width),
            full(CORES, groups, lines, width),
            full(CORES, chips, lines, width),
            full(chips, lines, width),
            full(chips, lines, width),
            full(chips, lines, width),
            full(depth, lines, width),
            full(levels, lines, width),
            full(lines, width),
            half(per, PARTS, chips, part, width),
            half(CORES, per, PARTS, chips, part, width),
            half(per, PARTS, chips, part, width),
            half(per, PARTS, chips, part, width),
            full(units, part, width),
            half(units, part, width),
            half(levels, units, part, width),
            half(per, PARTS, chips, part, width),
            half(per, PARTS, chips, part, width),
            half(per, PARTS, chips, part, width),
            half(per, PARTS, chips, part, width),
            half(per, PARTS, chips, part, width),
            dma(3), dma(per, 2),
            one, dma(per), one, one, one, dma(units), one, one,
            dma(max(depth - 1, 1)), dma(depth), dma(max(depth // 2, 1)), dma(levels, units),
            one, dma(units), one, dma(per),
            pltpu.SemaphoreType.REGULAR,
        ],
        compiler_params=pltpu.CompilerParams(
            collective_id=0, has_side_effects=True, vmem_limit_bytes=50 * 1024 * 1024
        ),
    )(*(pltpu.with_memory_space_constraint(a, pltpu.HBM) for a in arrays))


def solution(mesh):
    axes = ("outer", "narrow")
    block = P(axes, None)
    return jax.shard_map(
        functools.partial(on_device, tuple(mesh.shape[a] for a in axes)),
        mesh=mesh,
        in_specs=(block, block, block, P(None, axes), P()),
        out_specs=block,
        check_vma=False,
    )
```

```python
import functools

import jax
import jax.numpy as jnp
from jax import lax
from jax.experimental import pallas as pl
from jax.experimental.pallas import tpu as pltpu
from jax.sharding import PartitionSpec as P

MESH = pl.DeviceIdType.MESH
FAR = -1e30
CORES = 2
PARTS = 2
LAG_Z = 2
LAG_R = 6
BUSY = 3


def split_outer(outer):
    rows = 1
    for d in range(1, outer + 1):
        if d * d <= outer and outer % d == 0:
            rows = d
    return outer // rows, rows


def kernel(
    sizes, q_hbm, k_hbm, v_hbm, ld_hbm, gain_hbm, out_ref,
    q_ref, k_ref, v_ref, ld_ref, gain_ref, cum, cols_ref, grow_ref, tail_ref, side_ref, bias, inner, grown,
    tcore, dcore, ptot, tin, dchip, tz, dz,
    made, pair, tsend, got_t, q_sum, zsend, got_z, rsend, got_r, own_c, csend, got_c,
    load_sem, kv_sem, made_send, made_recv, ct_send, ct_recv, t_send, t_recv, pt_send, pt_recv,
    zt_send, zt_recv, z_send, z_recv, r_send, r_recv, c_send, c_recv, ready,
):
    depth, rows, across, heads, width, per = sizes
    chips = rows * across
    levels = max(depth - 1, 1).bit_length() if depth > 1 else 0
    tokens = q_ref.shape[0]
    part = width // PARTS
    units = per * PARTS
    unit = 4 if heads % 4 == 0 else 1
    groups = heads // unit
    o, n = lax.axis_index("outer"), lax.axis_index("narrow")
    z, y = o // rows, lax.rem(o, rows)
    x, core = n // CORES, lax.rem(n, CORES)
    me = y * across + x
    first = core == 0

    partner = (o, x * CORES + 1 - core)
    chip_at = lambda p: (z * rows + p // across, lax.rem(p, across) * CORES + core)
    plane_at = lambda j: (j * rows + y, n)
    beside = lambda i: lax.rem(y + i // across, rows) * across + lax.rem(x + i % across, across)
    back_slot = lambda i: (-(i // across) % rows) * across + -i % across - 1
    served = sorted(range(1, chips), key=lambda i: (-(i // across > 0) - (i % across > 0), i))

    def slot(p):
        i = lax.rem(p // across - y + rows, rows) * across + lax.rem(p % across - x + across, across)
        return lax.rem(i - 1 + chips, chips)


    def lanes(h, count=1):
        return pl.ds(pl.multiple_of(h * width, width), count * width)

    span = chips * CORES
    loads = [
        pltpu.make_async_copy(src, dst, load_sem.at[i])
        for i, (src, dst) in enumerate(((ld_hbm, ld_ref), (q_hbm, q_ref), (gain_hbm, gain_ref)))
    ]

    def load_kv(c):
        at = lanes(c * span, span)
        return [
            pltpu.make_async_copy(src.at[:, at], dst.at[:, at], kv_sem.at[c, i])
            for i, (src, dst) in enumerate(((k_hbm, k_ref), (v_hbm, v_ref)))
        ]

    loads[0].start()
    for one in load_kv(0):
        one.start()

    barrier = pltpu.get_barrier_semaphore()
    pl.semaphore_signal(barrier, inc=1, device_id=partner, device_id_type=MESH)
    for i in range(1, chips):
        pl.semaphore_signal(barrier, inc=1, device_id=chip_at(beside(i)), device_id_type=MESH)
    for j in range(1, depth):
        @pl.when(j > z)
        def _():
            pl.semaphore_signal(barrier, inc=1, device_id=plane_at(j), device_id_type=MESH)

    def remote(src, dst, send, recv, where):
        return pltpu.make_async_remote_copy(
            src_ref=src, dst_ref=dst, send_sem=send, recv_sem=recv, device_id=where, device_id_type=MESH
        )

    def arrived(ref, recv):
        remote(ref, ref, made_send, recv, partner).wait_recv()

    def sent(ref, send):
        remote(ref, ref, send, ct_recv, partner).wait_send()

    loads[0].wait()
    cols = jnp.concatenate([ld_ref[...], jnp.zeros((128 - heads, tokens), jnp.float32)], axis=0).T
    line = lax.broadcasted_iota(jnp.int32, cols.shape, 0)
    step = 1
    while step < tokens:
        if step < 8:
            moved = jnp.where(line >= step, pltpu.roll(cols, step, axis=0), 0.0)
        else:
            moved = jnp.concatenate([jnp.zeros((step, 128), jnp.float32), cols[: tokens - step]], axis=0)
        cols = cols + moved
        step *= 2
    cols_ref[...] = cols
    tcore[core] = cols[tokens - 1 :]
    tail = jnp.exp(cols[tokens - 1 :] - cols)
    side_ref[...] = pltpu.roll(tail, 127 + core, axis=1)
    tail_ref[...] = pltpu.roll(tail, lax.rem(128 - core, 128), axis=1)
    for c in range(1, per):
        for one in load_kv(c):
            one.start()
    loads[1].start()
    loads[2].start()

    def decay_rows():
        grow_ref[...] = jnp.exp(cols_ref[...])
        total = cols_ref[...].T[:heads]
        cum[...] = total
        at_t = lax.broadcasted_iota(jnp.int32, (width, width), 0)
        at_s = lax.broadcasted_iota(jnp.int32, (width, width), 1)
        bias[...] = jnp.where(at_t >= at_s, 0.0, FAR)

    def states(c, mine, some=None):
        a = core if mine else 1 - core
        tails = tail_ref if mine else side_ref
        for p in some or range(chips):
            u = c * span + p * CORES
            at = lanes(c * span + p * CORES + a)
            kept = k_ref[:, at].astype(jnp.float32) * tails[:, u : u + 1]
            made_here = lax.dot_general(
                kept.astype(jnp.bfloat16), v_ref[:, at], (((0,), (0,)), ((), ())),
                preferred_element_type=jnp.float32,
            ).astype(jnp.bfloat16)
            for f in range(PARTS):
                piece = made_here[f * part : (f + 1) * part]
                if mine:
                    pair[core, c, f, p] = piece
                else:
                    made[c, f, p] = piece

    def meet(c):
        arrived(pair.at[1 - core, c], made_recv.at[c])
        for f in range(PARTS):
            for p in range(chips):
                decay = dcore[c, p, 1:2, :]
                value = decay * pair[0, c, f, p].astype(jnp.float32) + pair[1, c, f, p].astype(jnp.float32)
                tsend[c, f, slot(p)] = value.astype(jnp.bfloat16)
            for i in served:
                remote(
                    tsend.at[c, f, i - 1], got_t.at[c, f, back_slot(i)], t_send,
                    t_recv.at[c * PARTS + f], chip_at(beside(i)),
                ).start()

    def spread_rows(rows, first_lane):
        count = -(-len(rows) // 8) * 8
        rows = rows + [jnp.zeros((count - len(rows), 128), jnp.float32)] * (count > len(rows))
        return pltpu.roll(jnp.exp(jnp.concatenate(rows, axis=0)), lax.rem(128 - first_lane, 128), axis=1)

    def meet_totals():
        arrived(tcore.at[1 - core], ct_recv)
        for i in range(chips):
            ptot[i] = tcore[0] + tcore[1]
        for i in served:
            remote(ptot.at[i - 1], tin.at[back_slot(i)], pt_send, pt_recv, chip_at(beside(i))).start()
        rows = spread_rows([tcore[k] for k in range(CORES)], core)
        pair_decays(rows, 0)
        return rows

    def pair_decays(rows, c):
        for p in range(chips):
            u = c * span + p * CORES
            dcore[c, p] = jnp.broadcast_to(rows[:, u : u + 1], (8, width))

    def within(g):
        for h in range(g * unit, (g + 1) * unit):
            at = slice(h * width, (h + 1) * width)
            column = jnp.broadcast_to(cols_ref[:, h : h + 1], (tokens, width))
            grown[h] = jnp.broadcast_to(grow_ref[:, h : h + 1], (tokens, width))
            row = cum[h : h + 1, :]
            scores = lax.dot_general(
                q_ref[:, at], k_ref[:, at], (((1,), (1,)), ((), ())),
                preferred_element_type=jnp.float32,
            )
            weights = []
            for t in range(tokens // width):
                rows_t = slice(t * width, (t + 1) * width)
                line = []
                for i in range(tokens // width):
                    at_i = slice(i * width, (i + 1) * width)
                    if i > t:
                        line.append(jnp.zeros((width, width), jnp.bfloat16))
                        continue
                    spread = column[rows_t] - row[:, at_i]
                    if i == t:
                        spread = spread + bias[...]
                    line.append((scores[rows_t, at_i] * jnp.exp(spread)).astype(jnp.bfloat16))
                weights.append(jnp.concatenate(line, axis=1))
            weights = jnp.concatenate(weights, axis=0)
            inner[:, at] = jnp.dot(weights, v_ref[:, at], preferred_element_type=jnp.float32)

    def send_level(level, s):
        for i in range(2**level):
            @pl.when(z + 1 + i < depth)
            def _():
                remote(
                    zsend.at[s], got_z.at[level, s], z_send.at[i], z_recv.at[level, s], plane_at(z + 1 + i)
                ).start()

    def sends_at(level):
        return lax.rem(z, 2 ** (level + 1)) == 2**level - 1

    def plane_totals():
        if chips > 1:
            arrived(tin.at[pl.ds(0, chips - 1)], pt_recv)
        tin[chips - 1] = ptot[chips - 1]
        rows = [tin[slot(p)] for p in range(chips)]
        whole = rows[0]
        for row in rows[1:]:
            whole = whole + row
        tz[z] = whole
        if depth > 1:
            @pl.when(z < depth - 1)
            def _():
                pl.semaphore_wait(ready, depth - 1 - z)
            for i in range(1, depth):
                @pl.when(z + i < depth)
                def _():
                    remote(tz.at[z], tz.at[z], zt_send.at[i - 1], zt_recv.at[z], plane_at(z + i)).start()
        rows = spread_rows(rows + [whole], me * CORES + core)
        for c in range(per):
            dchip[c] = jnp.broadcast_to(rows[:, c * span : c * span + 1], (rows.shape[0], width))

    def plane(s):
        c, f = s // PARTS, lax.rem(s, PARTS)
        if chips > 1:
            arrived(got_t.at[c, f, pl.ds(0, chips - 1)], t_recv.at[s])
        got_t[c, f, chips - 1] = tsend[c, f, chips - 1]
        acc = got_t[c, f, slot(0)].astype(jnp.float32)
        for p in range(1, chips):
            acc = dchip[c, p : p + 1, :] * acc + got_t[c, f, slot(p)].astype(jnp.float32)
        q_sum[s] = acc
        if levels:
            @pl.when(sends_at(0))
            def _():
                zsend[s] = acc.astype(jnp.bfloat16)
                send_level(0, s)

    def depth_totals():
        for j in range(depth - 1):
            @pl.when(j < z)
            def _():
                arrived(tz.at[j], zt_recv.at[j])
        rows = [jnp.zeros_like(tz[0])]
        for k in range(1, levels):
            start = z // 2**k * 2**k
            whole = jnp.zeros_like(tz[0])
            for j in range(depth - 1):
                whole = whole + jnp.where((j >= start) & (j < z), tz[j], 0.0)
            rows.append(whole)
        rows = spread_rows(rows, me * CORES + core)
        for c in range(per):
            dz[c] = jnp.broadcast_to(rows[:, c * span : c * span + 1], (rows.shape[0], width))

    def scan(s):
        c, f = s // PARTS, lax.rem(s, PARTS)
        acc = jnp.zeros((part, width), jnp.float32)
        for k in range(levels):
            odd = lax.rem(z // 2**k, 2) == 1

            @pl.when(odd)
            def _():
                arrived(got_z.at[k, s], z_recv.at[k, s])

            came = got_z[k, s].astype(jnp.float32)
            if k:
                came = dz[c, k : k + 1, :] * came + acc
            acc = jnp.where(odd, came, acc)
            if k + 1 < levels:
                @pl.when(sends_at(k + 1))
                def _():
                    zsend[s] = (dchip[c, chips : chips + 1, :] * acc + q_sum[s]).astype(jnp.bfloat16)
                    send_level(k + 1, s)
        for p in range(chips):
            rsend[c, f, slot(p)] = acc.astype(jnp.bfloat16)
            if p < chips - 1:
                acc = dchip[c, p : p + 1, :] * acc + got_t[c, f, slot(p)].astype(jnp.float32)
        for i in served:
            remote(
                rsend.at[c, f, i - 1], got_r.at[c, f, back_slot(i)], r_send, r_recv.at[s], chip_at(beside(i))
            ).start()

    def back(s):
        c, f = s // PARTS, lax.rem(s, PARTS)
        if chips > 1:
            arrived(got_r.at[c, f, pl.ds(0, chips - 1)], r_recv.at[s])
        got_r[c, f, chips - 1] = rsend[c, f, chips - 1]
        for p in range(chips):
            before = got_r[c, f, slot(p)]
            after = dcore[c, p, 0:1, :] * before.astype(jnp.float32) + pair[0, c, f, p].astype(jnp.float32)
            after = after.astype(jnp.bfloat16)
            own_c[c, f, p] = jnp.where(first, before, after)
            csend[c, f, p] = jnp.where(first, after, before)
        remote(csend.at[c, f], got_c.at[c, f], c_send, c_recv.at[c], partner).start()

    def finish(c, ref, a):
        for p in range(chips):
            h = c * span + p * CORES + a
            at = lanes(h)
            carried = jnp.concatenate([ref[c, f, p] for f in range(PARTS)], axis=0)
            read = jnp.dot(q_ref[:, at], carried, preferred_element_type=jnp.float32)
            numer = inner[:, at] + read * grown[h]
            mean = jnp.mean(numer * numer, axis=-1, keepdims=True)
            out_ref[:, at] = (numer * lax.rsqrt(mean + 1e-06) * gain_ref[:, at]).astype(jnp.bfloat16)

    for c in range(per):
        if c != 1:
            for one in load_kv(c):
                one.wait()
        states(c, False, range(chips // 2 if c == 1 else 0, chips))
        if c == 0:
            pl.semaphore_wait(barrier, chips + z)
            remote(tcore.at[core], tcore.at[core], ct_send, ct_recv, partner).start()
        remote(made.at[c], pair.at[core, c], made_send, made_recv.at[c], partner).start()
        if c == 0:
            for j in range(depth - 1):
                @pl.when(j < z)
                def _():
                    pl.semaphore_signal(ready, inc=1, device_id=plane_at(j), device_id_type=MESH)
            decay_rows()
        if c > 1:
            meet(c - 1)
        states(c, True)
        if c == 0 and per > 1:
            for one in load_kv(1):
                one.wait()
            states(1, False, range(chips // 2))
            pair_rows = meet_totals()
            meet(0)
            for later in range(1, per):
                pair_decays(pair_rows, later)
    if per == 1:
        meet_totals()
    loads[1].wait()
    loads[2].wait()
    plane_totals()
    within(0)
    meet(per - 1)


    rank = jnp.int32(0)
    for k in range(levels):
        rank = jnp.where(z >= 2**k, k + 1, rank)
    lag_z = jnp.minimum(jnp.where(rank == levels, units, jnp.where(rank == 0, 2 * LAG_Z, LAG_Z)), units)
    lag_r = lag_z + jnp.where(rank == levels, min(LAG_R, units), units)
    inner_planes = rank == levels
    slots = [jnp.where(inner_planes, g + g // 3, g if g < BUSY else max(g, units + LAG_Z + g - BUSY)) for g in range(groups - 1)]
    steps = jnp.maximum(lag_r + units, units + LAG_Z + groups)

    def step_at(s, _):
        @pl.when(s < units)
        def _():
            plane(s)

        if levels:
            @pl.when(s == lag_z)
            def _():
                depth_totals()

        @pl.when((s >= lag_z) & (s < lag_z + units))
        def _():
            scan(s - lag_z)

        @pl.when((s >= lag_r) & (s < lag_r + units))
        def _():
            back(s - lag_r)

        t = s - lag_r

        @pl.when((t >= 0) & (t < units - 1) & (lax.rem(t + units, PARTS) == PARTS - 1))
        def _():
            finish(t // PARTS, own_c, core)

        @pl.when((t >= 2 * PARTS) & (t < units - PARTS) & (lax.rem(t + units, PARTS) == 0))
        def _():
            c = (t - 2 * PARTS) // PARTS
            arrived(got_c.at[c], c_recv.at[c])
            finish(c, got_c, 1 - core)

        for g in range(1, groups):
            @pl.when(s == slots[g - 1])
            def _():
                within(g)

        return 0

    lax.fori_loop(0, steps, step_at, 0)
    finish(per - 1, own_c, core)
    for c in range(max(per - 3, 0), per):
        arrived(got_c.at[c], c_recv.at[c])
        finish(c, got_c, 1 - core)

    sent(made, made_send)
    sent(tcore.at[core], ct_send)
    if chips > 1:
        sent(tsend.at[:, :, pl.ds(0, chips - 1)], t_send)
        sent(ptot.at[pl.ds(0, chips - 1)], pt_send)
        sent(rsend.at[:, :, pl.ds(0, chips - 1)], r_send)
    sent(csend, c_send)
    for i in range(1, depth):
        @pl.when(z + i < depth)
        def _():
            sent(tz.at[z], zt_send.at[i - 1])
    for level in range(levels):
        for i in range(2**level):
            @pl.when(sends_at(level) & (z + 1 + i < depth))
            def _():
                sent(zsend, z_send.at[i])


def on_device(mesh_sizes, queries, keys, values, log_decay, gain):
    outer, narrow = mesh_sizes
    tokens, model = queries.shape
    heads = log_decay.shape[0]
    width = model // heads
    depth, rows = split_outer(outer)
    across = narrow // CORES
    chips = rows * across
    per = heads // (chips * CORES)
    groups = heads // per
    levels = max((depth - 1).bit_length(), 1)
    part = width // PARTS
    units = per * PARTS
    half = lambda *shape: pltpu.VMEM(shape, jnp.bfloat16)
    full = lambda *shape: pltpu.VMEM(shape, jnp.float32)
    dma = lambda *shape: pltpu.SemaphoreType.DMA(shape)
    one = pltpu.SemaphoreType.DMA
    vmem = pl.BlockSpec(memory_space=pltpu.VMEM)
    hbm = pl.BlockSpec(memory_space=pltpu.HBM)
    arrays = (queries, keys, values, log_decay, gain.reshape(1, model))
    return pl.pallas_call(
        functools.partial(kernel, (depth, rows, across, heads, width, per)),
        out_shape=jax.ShapeDtypeStruct(queries.shape, jnp.bfloat16),
        in_specs=[hbm] * 5,
        out_specs=vmem,
        scratch_shapes=[
            pltpu.VMEM((tokens, model), queries.dtype),
            pltpu.VMEM((tokens, model), queries.dtype),
            pltpu.VMEM((tokens, model), queries.dtype),
            full(heads, tokens),
            full(1, model),
            full(heads, tokens),
            full(tokens, 128),
            full(tokens, 128),
            full(tokens, 128),
            full(tokens, 128),
            full(width, width),
            full(tokens, model),
            full(heads, tokens, width),
            full(CORES, 1, 128),
            full(per, chips, 8, width),
            full(chips, 1, 128),
            full(chips, 1, 128),
            full(per, -(-(chips + 1) // 8) * 8, width),
            full(depth, 1, 128),
            full(per, -(-levels // 8) * 8, width),
            half(per, PARTS, chips, part, width),
            half(CORES, per, PARTS, chips, part, width),
            half(per, PARTS, chips, part, width),
            half(per, PARTS, chips, part, width),
            full(units, part, width),
            half(units, part, width),
            half(levels, units, part, width),
            half(per, PARTS, chips, part, width),
            half(per, PARTS, chips, part, width),
            half(per, PARTS, chips, part, width),
            half(per, PARTS, chips, part, width),
            half(per, PARTS, chips, part, width),
            dma(3), dma(per, 2),
            one, dma(per), one, one, one, dma(units), one, one,
            dma(max(depth - 1, 1)), dma(depth), dma(max(depth // 2, 1)), dma(levels, units),
            one, dma(units), one, dma(per),
            pltpu.SemaphoreType.REGULAR,
        ],
        compiler_params=pltpu.CompilerParams(
            collective_id=0, has_side_effects=True, vmem_limit_bytes=50 * 1024 * 1024
        ),
    )(*(pltpu.with_memory_space_constraint(a, pltpu.HBM) for a in arrays))


def solution(mesh):
    axes = ("outer", "narrow")
    block = P(axes, None)
    return jax.shard_map(
        functools.partial(on_device, tuple(mesh.shape[a] for a in axes)),
        mesh=mesh,
        in_specs=(block, block, block, P(None, axes), P()),
        out_specs=block,
        check_vma=False,
    )
```

```python
import functools

import jax
import jax.numpy as jnp
from jax import lax
from jax.experimental import pallas as pl
from jax.experimental.pallas import tpu as pltpu
from jax.sharding import PartitionSpec as P

MESH = pl.DeviceIdType.MESH
FAR = -1e30
CORES = 2
PARTS = 2
LAG_Z = 2
LAG_R = 6
BUSY = 3


def split_outer(outer):
    rows = 1
    for d in range(1, outer + 1):
        if d * d <= outer and outer % d == 0:
            rows = d
    return outer // rows, rows


def kernel(
    sizes, q_hbm, k_hbm, v_hbm, ld_hbm, gain_hbm, out_ref,
    q_ref, k_ref, v_ref, ld_ref, gain_ref, cum, cols_ref, grow_ref, tail_ref, side_ref, bias, inner, grown,
    tcore, dcore, ptot, tin, dchip, tz, dz,
    made, pair, tsend, got_t, q_sum, zsend, got_z, rsend, got_r, own_c, csend, got_c,
    load_sem, kv_sem, made_send, made_recv, ct_send, ct_recv, t_send, t_recv, pt_send, pt_recv,
    zt_send, zt_recv, z_send, z_recv, r_send, r_recv, c_send, c_recv, ready,
):
    depth, rows, across, heads, width, per = sizes
    chips = rows * across
    levels = max(depth - 1, 1).bit_length() if depth > 1 else 0
    tokens = q_ref.shape[0]
    part = width // PARTS
    units = per * PARTS
    unit = 4 if heads % 4 == 0 else 1
    groups = heads // unit
    o, n = lax.axis_index("outer"), lax.axis_index("narrow")
    z, y = o // rows, lax.rem(o, rows)
    x, core = n // CORES, lax.rem(n, CORES)
    me = y * across + x
    first = core == 0

    partner = (o, x * CORES + 1 - core)
    chip_at = lambda p: (z * rows + p // across, lax.rem(p, across) * CORES + core)
    plane_at = lambda j: (j * rows + y, n)
    beside = lambda i: lax.rem(y + i // across, rows) * across + lax.rem(x + i % across, across)
    back_slot = lambda i: (-(i // across) % rows) * across + -i % across - 1
    served = sorted(range(1, chips), key=lambda i: (-(i // across > 0) - (i % across > 0), i))

    def slot(p):
        i = lax.rem(p // across - y + rows, rows) * across + lax.rem(p % across - x + across, across)
        return lax.rem(i - 1 + chips, chips)


    def lanes(h, count=1):
        return pl.ds(pl.multiple_of(h * width, width), count * width)

    span = chips * CORES
    loads = [
        pltpu.make_async_copy(src, dst, load_sem.at[i])
        for i, (src, dst) in enumerate(((ld_hbm, ld_ref), (q_hbm, q_ref), (gain_hbm, gain_ref)))
    ]

    def load_kv(c):
        at = lanes(c * span, span)
        return [
            pltpu.make_async_copy(src.at[:, at], dst.at[:, at], kv_sem.at[c, i])
            for i, (src, dst) in enumerate(((k_hbm, k_ref), (v_hbm, v_ref)))
        ]

    loads[0].start()
    for one in load_kv(0):
        one.start()

    barrier = pltpu.get_barrier_semaphore()
    pl.semaphore_signal(barrier, inc=1, device_id=partner, device_id_type=MESH)
    for i in range(1, chips):
        pl.semaphore_signal(barrier, inc=1, device_id=chip_at(beside(i)), device_id_type=MESH)
    for j in range(1, depth):
        @pl.when(j > z)
        def _():
            pl.semaphore_signal(barrier, inc=1, device_id=plane_at(j), device_id_type=MESH)

    def remote(src, dst, send, recv, where):
        return pltpu.make_async_remote_copy(
            src_ref=src, dst_ref=dst, send_sem=send, recv_sem=recv, device_id=where, device_id_type=MESH
        )

    def arrived(ref, recv):
        remote(ref, ref, made_send, recv, partner).wait_recv()

    def sent(ref, send):
        remote(ref, ref, send, ct_recv, partner).wait_send()

    loads[0].wait()
    if per > 1:
        for one in load_kv(1):
            one.start()
    cols = jnp.concatenate([ld_ref[...], jnp.zeros((128 - heads, tokens), jnp.float32)], axis=0).T
    line = lax.broadcasted_iota(jnp.int32, cols.shape, 0)
    step = 1
    while step < tokens:
        if step < 8:
            moved = jnp.where(line >= step, pltpu.roll(cols, step, axis=0), 0.0)
        else:
            moved = jnp.concatenate([jnp.zeros((step, 128), jnp.float32), cols[: tokens - step]], axis=0)
        cols = cols + moved
        step *= 2
    cols_ref[...] = cols
    tcore[core] = cols[tokens - 1 :]
    tail = jnp.exp(cols[tokens - 1 :] - cols)
    side_ref[...] = pltpu.roll(tail, 127 + core, axis=1)
    tail_ref[...] = pltpu.roll(tail, lax.rem(128 - core, 128), axis=1)
    for c in range(2, per):
        for one in load_kv(c):
            one.start()
    loads[1].start()
    loads[2].start()

    def decay_rows():
        grow_ref[...] = jnp.exp(cols_ref[...])
        total = cols_ref[...].T[:heads]
        cum[...] = total
        at_t = lax.broadcasted_iota(jnp.int32, (width, width), 0)
        at_s = lax.broadcasted_iota(jnp.int32, (width, width), 1)
        bias[...] = jnp.where(at_t >= at_s, 0.0, FAR)

    def states(c, mine):
        a = core if mine else 1 - core
        tails = tail_ref if mine else side_ref
        for p in range(chips):
            u = c * span + p * CORES
            at = lanes(c * span + p * CORES + a)
            kept = k_ref[:, at].astype(jnp.float32) * tails[:, u : u + 1]
            made_here = lax.dot_general(
                kept.astype(jnp.bfloat16), v_ref[:, at], (((0,), (0,)), ((), ())),
                preferred_element_type=jnp.float32,
            ).astype(jnp.bfloat16)
            for f in range(PARTS):
                piece = made_here[f * part : (f + 1) * part]
                if mine:
                    pair[core, c, f, p] = piece
                else:
                    made[c, f, p] = piece

    def meet(c):
        arrived(pair.at[1 - core, c], made_recv.at[c])
        for f in range(PARTS):
            for p in range(chips):
                decay = dcore[c, p, 1:2, :]
                value = decay * pair[0, c, f, p].astype(jnp.float32) + pair[1, c, f, p].astype(jnp.float32)
                tsend[c, f, slot(p)] = value.astype(jnp.bfloat16)
            for i in served:
                remote(
                    tsend.at[c, f, i - 1], got_t.at[c, f, back_slot(i)], t_send,
                    t_recv.at[c * PARTS + f], chip_at(beside(i)),
                ).start()

    def spread_rows(rows, first_lane):
        count = -(-len(rows) // 8) * 8
        rows = rows + [jnp.zeros((count - len(rows), 128), jnp.float32)] * (count > len(rows))
        return pltpu.roll(jnp.exp(jnp.concatenate(rows, axis=0)), lax.rem(128 - first_lane, 128), axis=1)

    def meet_totals():
        arrived(tcore.at[1 - core], ct_recv)
        for i in range(chips):
            ptot[i] = tcore[0] + tcore[1]
        for i in served:
            remote(ptot.at[i - 1], tin.at[back_slot(i)], pt_send, pt_recv, chip_at(beside(i))).start()
        rows = spread_rows([tcore[k] for k in range(CORES)], core)
        pair_decays(rows, 0)
        return rows

    def pair_decays(rows, c):
        for p in range(chips):
            u = c * span + p * CORES
            dcore[c, p] = jnp.broadcast_to(rows[:, u : u + 1], (8, width))

    def within(g):
        for h in range(g * unit, (g + 1) * unit):
            at = slice(h * width, (h + 1) * width)
            column = jnp.broadcast_to(cols_ref[:, h : h + 1], (tokens, width))
            grown[h] = jnp.broadcast_to(grow_ref[:, h : h + 1], (tokens, width))
            row = cum[h : h + 1, :]
            scores = lax.dot_general(
                q_ref[:, at], k_ref[:, at], (((1,), (1,)), ((), ())),
                preferred_element_type=jnp.float32,
            )
            weights = []
            for t in range(tokens // width):
                rows_t = slice(t * width, (t + 1) * width)
                line = []
                for i in range(tokens // width):
                    at_i = slice(i * width, (i + 1) * width)
                    if i > t:
                        line.append(jnp.zeros((width, width), jnp.bfloat16))
                        continue
                    spread = column[rows_t] - row[:, at_i]
                    if i == t:
                        spread = spread + bias[...]
                    line.append((scores[rows_t, at_i] * jnp.exp(spread)).astype(jnp.bfloat16))
                weights.append(jnp.concatenate(line, axis=1))
            weights = jnp.concatenate(weights, axis=0)
            inner[:, at] = jnp.dot(weights, v_ref[:, at], preferred_element_type=jnp.float32)

    def send_level(level, s):
        for i in range(2**level):
            @pl.when(z + 1 + i < depth)
            def _():
                remote(
                    zsend.at[s], got_z.at[level, s], z_send.at[i], z_recv.at[level, s], plane_at(z + 1 + i)
                ).start()

    def sends_at(level):
        return lax.rem(z, 2 ** (level + 1)) == 2**level - 1

    def plane_totals():
        if chips > 1:
            arrived(tin.at[pl.ds(0, chips - 1)], pt_recv)
        tin[chips - 1] = ptot[chips - 1]
        rows = [tin[slot(p)] for p in range(chips)]
        whole = rows[0]
        for row in rows[1:]:
            whole = whole + row
        tz[z] = whole
        if depth > 1:
            @pl.when(z < depth - 1)
            def _():
                pl.semaphore_wait(ready, depth - 1 - z)
            for i in range(1, depth):
                @pl.when(z + i < depth)
                def _():
                    remote(tz.at[z], tz.at[z], zt_send.at[i - 1], zt_recv.at[z], plane_at(z + i)).start()
        rows = spread_rows(rows + [whole], me * CORES + core)
        for c in range(per):
            dchip[c] = jnp.broadcast_to(rows[:, c * span : c * span + 1], (rows.shape[0], width))

    def plane(s):
        c, f = s // PARTS, lax.rem(s, PARTS)
        if chips > 1:
            arrived(got_t.at[c, f, pl.ds(0, chips - 1)], t_recv.at[s])
        got_t[c, f, chips - 1] = tsend[c, f, chips - 1]
        acc = got_t[c, f, slot(0)].astype(jnp.float32)
        for p in range(1, chips):
            acc = dchip[c, p : p + 1, :] * acc + got_t[c, f, slot(p)].astype(jnp.float32)
        q_sum[s] = acc
        if levels:
            @pl.when(sends_at(0))
            def _():
                zsend[s] = acc.astype(jnp.bfloat16)
                send_level(0, s)

    def depth_totals():
        for j in range(depth - 1):
            @pl.when(j < z)
            def _():
                arrived(tz.at[j], zt_recv.at[j])
        rows = [jnp.zeros_like(tz[0])]
        for k in range(1, levels):
            start = z // 2**k * 2**k
            whole = jnp.zeros_like(tz[0])
            for j in range(depth - 1):
                whole = whole + jnp.where((j >= start) & (j < z), tz[j], 0.0)
            rows.append(whole)
        rows = spread_rows(rows, me * CORES + core)
        for c in range(per):
            dz[c] = jnp.broadcast_to(rows[:, c * span : c * span + 1], (rows.shape[0], width))

    def scan(s):
        c, f = s // PARTS, lax.rem(s, PARTS)
        acc = jnp.zeros((part, width), jnp.float32)
        for k in range(levels):
            odd = lax.rem(z // 2**k, 2) == 1

            @pl.when(odd)
            def _():
                arrived(got_z.at[k, s], z_recv.at[k, s])

            came = got_z[k, s].astype(jnp.float32)
            if k:
                came = dz[c, k : k + 1, :] * came + acc
            acc = jnp.where(odd, came, acc)
            if k + 1 < levels:
                @pl.when(sends_at(k + 1))
                def _():
                    zsend[s] = (dchip[c, chips : chips + 1, :] * acc + q_sum[s]).astype(jnp.bfloat16)
                    send_level(k + 1, s)
        for p in range(chips):
            rsend[c, f, slot(p)] = acc.astype(jnp.bfloat16)
            if p < chips - 1:
                acc = dchip[c, p : p + 1, :] * acc + got_t[c, f, slot(p)].astype(jnp.float32)
        for i in served:
            remote(
                rsend.at[c, f, i - 1], got_r.at[c, f, back_slot(i)], r_send, r_recv.at[s], chip_at(beside(i))
            ).start()

    def back(s):
        c, f = s // PARTS, lax.rem(s, PARTS)
        if chips > 1:
            arrived(got_r.at[c, f, pl.ds(0, chips - 1)], r_recv.at[s])
        got_r[c, f, chips - 1] = rsend[c, f, chips - 1]
        for p in range(chips):
            before = got_r[c, f, slot(p)]
            after = dcore[c, p, 0:1, :] * before.astype(jnp.float32) + pair[0, c, f, p].astype(jnp.float32)
            after = after.astype(jnp.bfloat16)
            own_c[c, f, p] = jnp.where(first, before, after)
            csend[c, f, p] = jnp.where(first, after, before)
        remote(csend.at[c, f], got_c.at[c, f], c_send, c_recv.at[c], partner).start()

    def finish(c, ref, a):
        for p in range(chips):
            h = c * span + p * CORES + a
            at = lanes(h)
            carried = jnp.concatenate([ref[c, f, p] for f in range(PARTS)], axis=0)
            read = jnp.dot(q_ref[:, at], carried, preferred_element_type=jnp.float32)
            numer = inner[:, at] + read * grown[h]
            mean = jnp.mean(numer * numer, axis=-1, keepdims=True)
            out_ref[:, at] = (numer * lax.rsqrt(mean + 1e-06) * gain_ref[:, at]).astype(jnp.bfloat16)

    def for_partner(c):
        for one in load_kv(c):
            one.wait()
        states(c, False)
        if c == 0:
            pl.semaphore_wait(barrier, chips + z)
            remote(tcore.at[core], tcore.at[core], ct_send, ct_recv, partner).start()
        remote(made.at[c], pair.at[core, c], made_send, made_recv.at[c], partner).start()

    for_partner(0)
    for j in range(depth - 1):
        @pl.when(j < z)
        def _():
            pl.semaphore_signal(ready, inc=1, device_id=plane_at(j), device_id_type=MESH)
    states(0, True)
    for c in range(1, per):
        for_partner(c)
        if c == 1:
            pair_rows = meet_totals()
        meet(c - 1)
        if c == 1:
            for later in range(1, per):
                pair_decays(pair_rows, later)
        states(c, True)
    if per == 1:
        meet_totals()
    decay_rows()
    loads[1].wait()
    loads[2].wait()
    plane_totals()
    within(0)
    meet(per - 1)

    rank = jnp.int32(0)
    for k in range(levels):
        rank = jnp.where(z >= 2**k, k + 1, rank)
    lag_z = jnp.minimum(jnp.where(rank == levels, units, jnp.where(rank == 0, 2 * LAG_Z, LAG_Z)), units)
    lag_r = lag_z + jnp.where(rank == levels, min(LAG_R, units), units)
    inner_planes = rank == levels
    slots = [jnp.where(inner_planes, g + g // 3 if g < units - 3 else 2 * g, g if g < BUSY else max(g, units + LAG_Z + g - BUSY)) for g in range(groups - 1)]
    steps = jnp.maximum(lag_r + units, max(units + LAG_Z + groups, 2 * groups))

    def step_at(s, _):
        @pl.when(s < units)
        def _():
            plane(s)

        if levels:
            @pl.when(s == lag_z)
            def _():
                depth_totals()

        @pl.when((s >= lag_z) & (s < lag_z + units))
        def _():
            scan(s - lag_z)

        @pl.when((s >= lag_r) & (s < lag_r + units))
        def _():
            back(s - lag_r)

        t = s - lag_r

        @pl.when((t >= 0) & (t < units - 1) & (lax.rem(t + units, PARTS) == PARTS - 1))
        def _():
            finish(t // PARTS, own_c, core)

        @pl.when((t >= 2 * PARTS) & (t < units - PARTS) & (lax.rem(t + units, PARTS) == 0))
        def _():
            c = (t - 2 * PARTS) // PARTS
            arrived(got_c.at[c], c_recv.at[c])
            finish(c, got_c, 1 - core)

        for g in range(1, groups):
            @pl.when(s == slots[g - 1])
            def _():
                within(g)

        return 0

    lax.fori_loop(0, steps, step_at, 0)
    finish(per - 1, own_c, core)
    for c in range(max(per - 3, 0), per):
        arrived(got_c.at[c], c_recv.at[c])
        finish(c, got_c, 1 - core)

    sent(made, made_send)
    sent(tcore.at[core], ct_send)
    if chips > 1:
        sent(tsend.at[:, :, pl.ds(0, chips - 1)], t_send)
        sent(ptot.at[pl.ds(0, chips - 1)], pt_send)
        sent(rsend.at[:, :, pl.ds(0, chips - 1)], r_send)
    sent(csend, c_send)
    for i in range(1, depth):
        @pl.when(z + i < depth)
        def _():
            sent(tz.at[z], zt_send.at[i - 1])
    for level in range(levels):
        for i in range(2**level):
            @pl.when(sends_at(level) & (z + 1 + i < depth))
            def _():
                sent(zsend, z_send.at[i])


def on_device(mesh_sizes, queries, keys, values, log_decay, gain):
    outer, narrow = mesh_sizes
    tokens, model = queries.shape
    heads = log_decay.shape[0]
    width = model // heads
    depth, rows = split_outer(outer)
    across = narrow // CORES
    chips = rows * across
    per = heads // (chips * CORES)
    groups = heads // per
    levels = max((depth - 1).bit_length(), 1)
    part = width // PARTS
    units = per * PARTS
    half = lambda *shape: pltpu.VMEM(shape, jnp.bfloat16)
    full = lambda *shape: pltpu.VMEM(shape, jnp.float32)
    dma = lambda *shape: pltpu.SemaphoreType.DMA(shape)
    one = pltpu.SemaphoreType.DMA
    vmem = pl.BlockSpec(memory_space=pltpu.VMEM)
    hbm = pl.BlockSpec(memory_space=pltpu.HBM)
    arrays = (queries, keys, values, log_decay, gain.reshape(1, model))
    return pl.pallas_call(
        functools.partial(kernel, (depth, rows, across, heads, width, per)),
        out_shape=jax.ShapeDtypeStruct(queries.shape, jnp.bfloat16),
        in_specs=[hbm] * 5,
        out_specs=vmem,
        scratch_shapes=[
            pltpu.VMEM((tokens, model), queries.dtype),
            pltpu.VMEM((tokens, model), queries.dtype),
            pltpu.VMEM((tokens, model), queries.dtype),
            full(heads, tokens),
            full(1, model),
            full(heads, tokens),
            full(tokens, 128),
            full(tokens, 128),
            full(tokens, 128),
            full(tokens, 128),
            full(width, width),
            full(tokens, model),
            full(heads, tokens, width),
            full(CORES, 1, 128),
            full(per, chips, 8, width),
            full(chips, 1, 128),
            full(chips, 1, 128),
            full(per, -(-(chips + 1) // 8) * 8, width),
            full(depth, 1, 128),
            full(per, -(-levels // 8) * 8, width),
            half(per, PARTS, chips, part, width),
            half(CORES, per, PARTS, chips, part, width),
            half(per, PARTS, chips, part, width),
            half(per, PARTS, chips, part, width),
            full(units, part, width),
            half(units, part, width),
            half(levels, units, part, width),
            half(per, PARTS, chips, part, width),
            half(per, PARTS, chips, part, width),
            half(per, PARTS, chips, part, width),
            half(per, PARTS, chips, part, width),
            half(per, PARTS, chips, part, width),
            dma(3), dma(per, 2),
            one, dma(per), one, one, one, dma(units), one, one,
            dma(max(depth - 1, 1)), dma(depth), dma(max(depth // 2, 1)), dma(levels, units),
            one, dma(units), one, dma(per),
            pltpu.SemaphoreType.REGULAR,
        ],
        compiler_params=pltpu.CompilerParams(
            collective_id=0, has_side_effects=True, vmem_limit_bytes=50 * 1024 * 1024
        ),
    )(*(pltpu.with_memory_space_constraint(a, pltpu.HBM) for a in arrays))


def solution(mesh):
    axes = ("outer", "narrow")
    block = P(axes, None)
    return jax.shard_map(
        functools.partial(on_device, tuple(mesh.shape[a] for a in axes)),
        mesh=mesh,
        in_specs=(block, block, block, P(None, axes), P()),
        out_specs=block,
        check_vma=False,
    )
```

```python
import functools

import jax
import jax.numpy as jnp
from jax import lax
from jax.experimental import pallas as pl
from jax.experimental.pallas import tpu as pltpu
from jax.sharding import PartitionSpec as P

MESH = pl.DeviceIdType.MESH
FAR = -1e30
CORES = 2
PARTS = 2
LAG_Z = 2
LAG_R = 7
BUSY = 3


def split_outer(outer):
    rows = 1
    for d in range(1, outer + 1):
        if d * d <= outer and outer % d == 0:
            rows = d
    return outer // rows, rows


def kernel(
    sizes, q_hbm, k_hbm, v_hbm, ld_hbm, gain_hbm, out_ref,
    q_ref, k_ref, v_ref, ld_ref, gain_ref, cum, cols_ref, grow_ref, tail_ref, side_ref, bias, inner, grown,
    tcore, dcore, ptot, tin, dchip, tz, dz,
    made, pair, tsend, got_t, q_sum, zsend, got_z, rsend, got_r, own_c, csend, got_c,
    load_sem, kv_sem, made_send, made_recv, ct_send, ct_recv, t_send, t_recv, pt_send, pt_recv,
    zt_send, zt_recv, z_send, z_recv, r_send, r_recv, c_send, c_recv, ready,
):
    depth, rows, across, heads, width, per = sizes
    chips = rows * across
    levels = max(depth - 1, 1).bit_length() if depth > 1 else 0
    tokens = q_ref.shape[0]
    part = width // PARTS
    units = per * PARTS
    unit = 4 if heads % 4 == 0 else 1
    groups = heads // unit
    o, n = lax.axis_index("outer"), lax.axis_index("narrow")
    z, y = o // rows, lax.rem(o, rows)
    x, core = n // CORES, lax.rem(n, CORES)
    me = y * across + x
    first = core == 0

    partner = (o, x * CORES + 1 - core)
    chip_at = lambda p: (z * rows + p // across, lax.rem(p, across) * CORES + core)
    plane_at = lambda j: (j * rows + y, n)
    beside = lambda i: lax.rem(y + i // across, rows) * across + lax.rem(x + i % across, across)
    back_slot = lambda i: (-(i // across) % rows) * across + -i % across - 1
    served = sorted(range(1, chips), key=lambda i: (-(i // across > 0) - (i % across > 0), i))

    def slot(p):
        i = lax.rem(p // across - y + rows, rows) * across + lax.rem(p % across - x + across, across)
        return lax.rem(i - 1 + chips, chips)


    def lanes(h, count=1):
        return pl.ds(pl.multiple_of(h * width, width), count * width)

    span = chips * CORES
    loads = [
        pltpu.make_async_copy(src, dst, load_sem.at[i])
        for i, (src, dst) in enumerate(((ld_hbm, ld_ref), (q_hbm, q_ref), (gain_hbm, gain_ref)))
    ]

    def load_kv(c):
        at = lanes(c * span, span)
        return [
            pltpu.make_async_copy(src.at[:, at], dst.at[:, at], kv_sem.at[c, i])
            for i, (src, dst) in enumerate(((k_hbm, k_ref), (v_hbm, v_ref)))
        ]

    loads[0].start()
    for one in load_kv(0):
        one.start()

    barrier = pltpu.get_barrier_semaphore()
    pl.semaphore_signal(barrier, inc=1, device_id=partner, device_id_type=MESH)
    for i in range(1, chips):
        pl.semaphore_signal(barrier, inc=1, device_id=chip_at(beside(i)), device_id_type=MESH)
    for j in range(1, depth):
        @pl.when(j > z)
        def _():
            pl.semaphore_signal(barrier, inc=1, device_id=plane_at(j), device_id_type=MESH)

    def remote(src, dst, send, recv, where):
        return pltpu.make_async_remote_copy(
            src_ref=src, dst_ref=dst, send_sem=send, recv_sem=recv, device_id=where, device_id_type=MESH
        )

    def arrived(ref, recv):
        remote(ref, ref, made_send, recv, partner).wait_recv()

    def sent(ref, send):
        remote(ref, ref, send, ct_recv, partner).wait_send()

    loads[0].wait()
    if per > 1:
        for one in load_kv(1):
            one.start()
    cols = jnp.concatenate([ld_ref[...], jnp.zeros((128 - heads, tokens), jnp.float32)], axis=0).T
    line = lax.broadcasted_iota(jnp.int32, cols.shape, 0)
    step = 1
    while step < tokens:
        if step < 8:
            moved = jnp.where(line >= step, pltpu.roll(cols, step, axis=0), 0.0)
        else:
            moved = jnp.concatenate([jnp.zeros((step, 128), jnp.float32), cols[: tokens - step]], axis=0)
        cols = cols + moved
        step *= 2
    cols_ref[...] = cols
    tcore[core] = cols[tokens - 1 :]
    tail = jnp.exp(cols[tokens - 1 :] - cols)
    side_ref[...] = pltpu.roll(tail, 127 + core, axis=1)
    tail_ref[...] = pltpu.roll(tail, lax.rem(128 - core, 128), axis=1)
    for c in range(2, per):
        for one in load_kv(c):
            one.start()
    loads[1].start()
    loads[2].start()

    def decay_rows():
        grow_ref[...] = jnp.exp(cols_ref[...])
        total = cols_ref[...].T[:heads]
        cum[...] = total
        at_t = lax.broadcasted_iota(jnp.int32, (width, width), 0)
        at_s = lax.broadcasted_iota(jnp.int32, (width, width), 1)
        bias[...] = jnp.where(at_t >= at_s, 0.0, FAR)

    def states(c, mine):
        a = core if mine else 1 - core
        tails = tail_ref if mine else side_ref
        for p in range(chips):
            u = c * span + p * CORES
            at = lanes(c * span + p * CORES + a)
            kept = k_ref[:, at].astype(jnp.float32) * tails[:, u : u + 1]
            made_here = lax.dot_general(
                kept.astype(jnp.bfloat16), v_ref[:, at], (((0,), (0,)), ((), ())),
                preferred_element_type=jnp.float32,
            ).astype(jnp.bfloat16)
            for f in range(PARTS):
                piece = made_here[f * part : (f + 1) * part]
                if mine:
                    pair[core, c, f, p] = piece
                else:
                    made[c, f, p] = piece

    def meet(c):
        arrived(pair.at[1 - core, c], made_recv.at[c])
        for f in range(PARTS):
            for p in range(chips):
                decay = dcore[c, p, 1:2, :]
                value = decay * pair[0, c, f, p].astype(jnp.float32) + pair[1, c, f, p].astype(jnp.float32)
                tsend[c, f, slot(p)] = value.astype(jnp.bfloat16)
            for i in served:
                remote(
                    tsend.at[c, f, i - 1], got_t.at[c, f, back_slot(i)], t_send,
                    t_recv.at[c * PARTS + f], chip_at(beside(i)),
                ).start()

    def spread_rows(rows, first_lane):
        count = -(-len(rows) // 8) * 8
        rows = rows + [jnp.zeros((count - len(rows), 128), jnp.float32)] * (count > len(rows))
        return pltpu.roll(jnp.exp(jnp.concatenate(rows, axis=0)), lax.rem(128 - first_lane, 128), axis=1)

    def meet_totals():
        arrived(tcore.at[1 - core], ct_recv)
        for i in range(chips):
            ptot[i] = tcore[0] + tcore[1]
        for i in served:
            remote(ptot.at[i - 1], tin.at[back_slot(i)], pt_send, pt_recv, chip_at(beside(i))).start()
        rows = spread_rows([tcore[k] for k in range(CORES)], core)
        pair_decays(rows, 0)
        return rows

    def pair_decays(rows, c):
        for p in range(chips):
            u = c * span + p * CORES
            dcore[c, p] = jnp.broadcast_to(rows[:, u : u + 1], (8, width))

    def within(g):
        for h in range(g * unit, (g + 1) * unit):
            at = slice(h * width, (h + 1) * width)
            column = jnp.broadcast_to(cols_ref[:, h : h + 1], (tokens, width))
            grown[h] = jnp.broadcast_to(grow_ref[:, h : h + 1], (tokens, width))
            row = cum[h : h + 1, :]
            scores = lax.dot_general(
                q_ref[:, at], k_ref[:, at], (((1,), (1,)), ((), ())),
                preferred_element_type=jnp.float32,
            )
            weights = []
            for t in range(tokens // width):
                rows_t = slice(t * width, (t + 1) * width)
                line = []
                for i in range(tokens // width):
                    at_i = slice(i * width, (i + 1) * width)
                    if i > t:
                        line.append(jnp.zeros((width, width), jnp.bfloat16))
                        continue
                    spread = column[rows_t] - row[:, at_i]
                    if i == t:
                        spread = spread + bias[...]
                    line.append((scores[rows_t, at_i] * jnp.exp(spread)).astype(jnp.bfloat16))
                weights.append(jnp.concatenate(line, axis=1))
            weights = jnp.concatenate(weights, axis=0)
            inner[:, at] = jnp.dot(weights, v_ref[:, at], preferred_element_type=jnp.float32)

    def send_level(level, s):
        for i in range(2**level):
            @pl.when(z + 1 + i < depth)
            def _():
                remote(
                    zsend.at[s], got_z.at[level, s], z_send.at[i], z_recv.at[level, s], plane_at(z + 1 + i)
                ).start()

    def sends_at(level):
        return lax.rem(z, 2 ** (level + 1)) == 2**level - 1

    def plane_totals():
        if chips > 1:
            arrived(tin.at[pl.ds(0, chips - 1)], pt_recv)
        tin[chips - 1] = ptot[chips - 1]
        rows = [tin[slot(p)] for p in range(chips)]
        whole = rows[0]
        for row in rows[1:]:
            whole = whole + row
        tz[z] = whole
        if depth > 1:
            @pl.when(z < depth - 1)
            def _():
                pl.semaphore_wait(ready, depth - 1 - z)
            for i in range(1, depth):
                @pl.when(z + i < depth)
                def _():
                    remote(tz.at[z], tz.at[z], zt_send.at[i - 1], zt_recv.at[z], plane_at(z + i)).start()
        rows = spread_rows(rows + [whole], me * CORES + core)
        for c in range(per):
            dchip[c] = jnp.broadcast_to(rows[:, c * span : c * span + 1], (rows.shape[0], width))

    def plane(s):
        c, f = s // PARTS, lax.rem(s, PARTS)
        if chips > 1:
            arrived(got_t.at[c, f, pl.ds(0, chips - 1)], t_recv.at[s])
        got_t[c, f, chips - 1] = tsend[c, f, chips - 1]
        acc = got_t[c, f, slot(0)].astype(jnp.float32)
        for p in range(1, chips):
            acc = dchip[c, p : p + 1, :] * acc + got_t[c, f, slot(p)].astype(jnp.float32)
        q_sum[s] = acc
        if levels:
            @pl.when(sends_at(0))
            def _():
                zsend[s] = acc.astype(jnp.bfloat16)
                send_level(0, s)

    def depth_totals():
        for j in range(depth - 1):
            @pl.when(j < z)
            def _():
                arrived(tz.at[j], zt_recv.at[j])
        rows = [jnp.zeros_like(tz[0])]
        for k in range(1, levels):
            start = z // 2**k * 2**k
            whole = jnp.zeros_like(tz[0])
            for j in range(depth - 1):
                whole = whole + jnp.where((j >= start) & (j < z), tz[j], 0.0)
            rows.append(whole)
        rows = spread_rows(rows, me * CORES + core)
        for c in range(per):
            dz[c] = jnp.broadcast_to(rows[:, c * span : c * span + 1], (rows.shape[0], width))

    def scan(s):
        c, f = s // PARTS, lax.rem(s, PARTS)
        acc = jnp.zeros((part, width), jnp.float32)
        for k in range(levels):
            odd = lax.rem(z // 2**k, 2) == 1

            @pl.when(odd)
            def _():
                arrived(got_z.at[k, s], z_recv.at[k, s])

            came = got_z[k, s].astype(jnp.float32)
            if k:
                came = dz[c, k : k + 1, :] * came + acc
            acc = jnp.where(odd, came, acc)
            if k + 1 < levels:
                @pl.when(sends_at(k + 1))
                def _():
                    zsend[s] = (dchip[c, chips : chips + 1, :] * acc + q_sum[s]).astype(jnp.bfloat16)
                    send_level(k + 1, s)
        for p in range(chips):
            rsend[c, f, slot(p)] = acc.astype(jnp.bfloat16)
            if p < chips - 1:
                acc = dchip[c, p : p + 1, :] * acc + got_t[c, f, slot(p)].astype(jnp.float32)
        for i in served:
            remote(
                rsend.at[c, f, i - 1], got_r.at[c, f, back_slot(i)], r_send, r_recv.at[s], chip_at(beside(i))
            ).start()

    def back(s):
        c, f = s // PARTS, lax.rem(s, PARTS)
        if chips > 1:
            arrived(got_r.at[c, f, pl.ds(0, chips - 1)], r_recv.at[s])
        got_r[c, f, chips - 1] = rsend[c, f, chips - 1]
        for p in range(chips):
            before = got_r[c, f, slot(p)]
            after = dcore[c, p, 0:1, :] * before.astype(jnp.float32) + pair[0, c, f, p].astype(jnp.float32)
            after = after.astype(jnp.bfloat16)
            own_c[c, f, p] = jnp.where(first, before, after)
            csend[c, f, p] = jnp.where(first, after, before)
        remote(csend.at[c, f], got_c.at[c, f], c_send, c_recv.at[c], partner).start()

    def finish(c, ref, a):
        for p in range(chips):
            h = c * span + p * CORES + a
            at = lanes(h)
            carried = jnp.concatenate([ref[c, f, p] for f in range(PARTS)], axis=0)
            read = jnp.dot(q_ref[:, at], carried, preferred_element_type=jnp.float32)
            numer = inner[:, at] + read * grown[h]
            mean = jnp.mean(numer * numer, axis=-1, keepdims=True)
            out_ref[:, at] = (numer * lax.rsqrt(mean + 1e-06) * gain_ref[:, at]).astype(jnp.bfloat16)

    def for_partner(c):
        for one in load_kv(c):
            one.wait()
        states(c, False)
        if c == 0:
            pl.semaphore_wait(barrier, chips + z)
            remote(tcore.at[core], tcore.at[core], ct_send, ct_recv, partner).start()
        remote(made.at[c], pair.at[core, c], made_send, made_recv.at[c], partner).start()

    for_partner(0)
    for j in range(depth - 1):
        @pl.when(j < z)
        def _():
            pl.semaphore_signal(ready, inc=1, device_id=plane_at(j), device_id_type=MESH)
    states(0, True)
    for c in range(1, per):
        for_partner(c)
        if c == 1:
            pair_rows = meet_totals()
        meet(c - 1)
        if c == 1:
            for later in range(1, per):
                pair_decays(pair_rows, later)
        states(c, True)
    if per == 1:
        meet_totals()
    decay_rows()
    loads[1].wait()
    loads[2].wait()
    plane_totals()
    within(0)
    meet(per - 1)

    rank = jnp.int32(0)
    for k in range(levels):
        rank = jnp.where(z >= 2**k, k + 1, rank)
    lag_z = jnp.minimum(jnp.where(rank == levels, units, jnp.where(rank == 0, 2 * LAG_Z, LAG_Z)), units)
    lag_r = lag_z + jnp.where(rank == levels, min(LAG_R, units), units)
    inner_planes = rank == levels
    slots = [jnp.where(inner_planes, g + g // 3 if g < units - 3 else 2 * g, g if g < BUSY else max(g, units + LAG_Z + g - BUSY)) for g in range(groups - 1)]
    steps = jnp.maximum(lag_r + units, max(units + LAG_Z + groups, 2 * groups))

    def step_at(s, _):
        @pl.when(s < units)
        def _():
            plane(s)

        if levels:
            @pl.when(s == lag_z)
            def _():
                depth_totals()

        @pl.when((s >= lag_z) & (s < lag_z + units))
        def _():
            scan(s - lag_z)

        @pl.when((s >= lag_r) & (s < lag_r + units))
        def _():
            back(s - lag_r)

        t = s - lag_r

        @pl.when((t >= 0) & (t < units - 1) & (lax.rem(t + units, PARTS) == PARTS - 1))
        def _():
            finish(t // PARTS, own_c, core)

        @pl.when((t >= 2 * PARTS) & (t < units - PARTS) & (lax.rem(t + units, PARTS) == 0))
        def _():
            c = (t - 2 * PARTS) // PARTS
            arrived(got_c.at[c], c_recv.at[c])
            finish(c, got_c, 1 - core)

        for g in range(1, groups):
            @pl.when(s == slots[g - 1])
            def _():
                within(g)

        return 0

    lax.fori_loop(0, steps, step_at, 0)
    finish(per - 1, own_c, core)
    for c in range(max(per - 3, 0), per):
        arrived(got_c.at[c], c_recv.at[c])
        finish(c, got_c, 1 - core)

    sent(made, made_send)
    sent(tcore.at[core], ct_send)
    if chips > 1:
        sent(tsend.at[:, :, pl.ds(0, chips - 1)], t_send)
        sent(ptot.at[pl.ds(0, chips - 1)], pt_send)
        sent(rsend.at[:, :, pl.ds(0, chips - 1)], r_send)
    sent(csend, c_send)
    for i in range(1, depth):
        @pl.when(z + i < depth)
        def _():
            sent(tz.at[z], zt_send.at[i - 1])
    for level in range(levels):
        for i in range(2**level):
            @pl.when(sends_at(level) & (z + 1 + i < depth))
            def _():
                sent(zsend, z_send.at[i])


def on_device(mesh_sizes, queries, keys, values, log_decay, gain):
    outer, narrow = mesh_sizes
    tokens, model = queries.shape
    heads = log_decay.shape[0]
    width = model // heads
    depth, rows = split_outer(outer)
    across = narrow // CORES
    chips = rows * across
    per = heads // (chips * CORES)
    groups = heads // per
    levels = max((depth - 1).bit_length(), 1)
    part = width // PARTS
    units = per * PARTS
    half = lambda *shape: pltpu.VMEM(shape, jnp.bfloat16)
    full = lambda *shape: pltpu.VMEM(shape, jnp.float32)
    dma = lambda *shape: pltpu.SemaphoreType.DMA(shape)
    one = pltpu.SemaphoreType.DMA
    vmem = pl.BlockSpec(memory_space=pltpu.VMEM)
    hbm = pl.BlockSpec(memory_space=pltpu.HBM)
    arrays = (queries, keys, values, log_decay, gain.reshape(1, model))
    return pl.pallas_call(
        functools.partial(kernel, (depth, rows, across, heads, width, per)),
        out_shape=jax.ShapeDtypeStruct(queries.shape, jnp.bfloat16),
        in_specs=[hbm] * 5,
        out_specs=vmem,
        scratch_shapes=[
            pltpu.VMEM((tokens, model), queries.dtype),
            pltpu.VMEM((tokens, model), queries.dtype),
            pltpu.VMEM((tokens, model), queries.dtype),
            full(heads, tokens),
            full(1, model),
            full(heads, tokens),
            full(tokens, 128),
            full(tokens, 128),
            full(tokens, 128),
            full(tokens, 128),
            full(width, width),
            full(tokens, model),
            full(heads, tokens, width),
            full(CORES, 1, 128),
            full(per, chips, 8, width),
            full(chips, 1, 128),
            full(chips, 1, 128),
            full(per, -(-(chips + 1) // 8) * 8, width),
            full(depth, 1, 128),
            full(per, -(-levels // 8) * 8, width),
            half(per, PARTS, chips, part, width),
            half(CORES, per, PARTS, chips, part, width),
            half(per, PARTS, chips, part, width),
            half(per, PARTS, chips, part, width),
            full(units, part, width),
            half(units, part, width),
            half(levels, units, part, width),
            half(per, PARTS, chips, part, width),
            half(per, PARTS, chips, part, width),
            half(per, PARTS, chips, part, width),
            half(per, PARTS, chips, part, width),
            half(per, PARTS, chips, part, width),
            dma(3), dma(per, 2),
            one, dma(per), one, one, one, dma(units), one, one,
            dma(max(depth - 1, 1)), dma(depth), dma(max(depth // 2, 1)), dma(levels, units),
            one, dma(units), one, dma(per),
            pltpu.SemaphoreType.REGULAR,
        ],
        compiler_params=pltpu.CompilerParams(
            collective_id=0, has_side_effects=True, vmem_limit_bytes=50 * 1024 * 1024
        ),
    )(*(pltpu.with_memory_space_constraint(a, pltpu.HBM) for a in arrays))


def solution(mesh):
    axes = ("outer", "narrow")
    block = P(axes, None)
    return jax.shard_map(
        functools.partial(on_device, tuple(mesh.shape[a] for a in axes)),
        mesh=mesh,
        in_specs=(block, block, block, P(None, axes), P()),
        out_specs=block,
        check_vma=False,
    )
```
